512 devices in a mesh: dp: 32 (over x, y, core), seq: 16 (over z).
Axes of the slice: x: 4, y: 4, z: 16, core: 2. Of those that a mesh axis runs over, the one named last changes fastest.
Arguments:
- tiles: bfloat16 [16384, 2, 8, 8, 192], P(('dp', 'seq')), may hold values from -6 to 6
- tile_dest: int32 [16384], P(('dp', 'seq')), may hold values from 0 to 31, as said below
- tile_meta: int32 [16384, 4], P(('dp', 'seq')), may hold values from 0 to 63, as said below
- space_weight: bfloat16 [1728, 192], replicated, may hold values from -0.15625 to 0.15625
- time_weight: bfloat16 [576, 192], replicated, may hold values from -0.25 to 0.25
- conv_bias: float32 [192], replicated, may hold values from -3 to 3
- latent_weight: bfloat16 [192, 16], replicated, may hold values from -0.4375 to 0.4375
- embed_weight: bfloat16 [64, 5120], replicated, may hold values from -0.75 to 0.75
- qkv_weight: bfloat16 [5120, 384], P('seq'), may hold values from -2 to 2
- rope_freq: float32 [64], replicated, may hold values from 0.05 to 1
- cotangent: bfloat16 [131072, 128], P(('dp', 'seq')), may hold values from -16 to 16
Outputs:
- attended: bfloat16 [131072, 128], P(('dp', 'seq'))
- freq_grad: float32 [64], replicated
The draws below stay inside these ranges and needn't reach their ends.
Inputs may be any that keep to these rules, and one draw needn't show every extreme that they name: `tile_dest`: among the tiles of one device, at most 2 name one dp index. Every owner receives at most 64 tiles; in every draw, in every seq index, some owner receives exactly 64, 2 from every loader. `tile_meta`: column 0 numbers the tiles of one owner 0, 1, 2 and so on without gaps; columns 1 to 3 are not negative and below 64.
All inputs are finite; a program needn't handle non-finite values.
Results may differ from the reference program's by a relative error of at most 0.034.
Values may be sent and summed in bfloat16 or wider, within the bound.
A program may use at most 128 MiB of HBM per device.

```python
import math
import jax
import jax.numpy as jnp
from jax import lax

TILES_DEV = 32
TILE_F = 2
TILE_H = 8
TILE_W = 8
CH = 192
LAT = 16
D = 5120
HD = 128
HEADS = 1
GRID_H = 4
PATCH = 64
PAIRS = 64
OWN_MAX = 64
KEYS = 4096
TILES_ALL = 16384
ROWS = 131072
N_DP = 32
N_SEQ = 16


def tile_layout(key):
    base_key = jax.random.fold_in(key, 11)
    width_key = jax.random.fold_in(base_key, 1)
    grid_wide = 2 + jax.random.randint(width_key, (N_DP,), 0, 7)

    def one_column(column_id):
        column_key = jax.random.fold_in(base_key, 100 + column_id)
        pair_key = jax.random.fold_in(column_key, 1)
        size_key = jax.random.fold_in(column_key, 2)
        order_key = jax.random.fold_in(column_key, 3)
        pairing = jax.random.permutation(pair_key, N_DP)
        extra = jax.random.randint(size_key, (N_DP // 2,), 0, TILES_DEV + 1)
        extra = extra.at[0].set(TILES_DEV)
        counts = jnp.zeros((N_DP,), jnp.int32)
        counts = counts.at[pairing[0::2]].set(TILES_DEV + extra)
        counts = counts.at[pairing[1::2]].set(TILES_DEV - extra)
        ends = jnp.cumsum(counts)
        starts = ends - counts
        entry = jnp.arange(N_DP * TILES_DEV, dtype=jnp.int32)
        owner = jnp.searchsorted(ends, entry, side='right').astype(jnp.int32)
        rank_in = entry - starts[owner]

        def shuffle_one(loader_key):
            return jax.random.permutation(loader_key, TILES_DEV)
        shuffles = jax.vmap(shuffle_one)(jax.random.split(order_key, N_DP))
        picked = shuffles * N_DP + jnp.arange(N_DP, dtype=jnp.int32)[:, None]
        dest_ids = owner[picked]
        position = rank_in[picked]
        wide = grid_wide[dest_ids]
        frame_idx = position // (wide * GRID_H)
        row_idx = position // wide % GRID_H
        col_idx = position % wide
        meta_rows = jnp.stack([position, frame_idx, row_idx, col_idx], axis=-1)
        return (dest_ids, meta_rows)
    dest_all, meta_all = jax.vmap(one_column)(jnp.arange(N_SEQ, dtype=jnp.int32))
    dest_all = dest_all.transpose(1, 0, 2).reshape(TILES_ALL)
    meta_all = meta_all.transpose(1, 0, 2, 3).reshape(TILES_ALL, 4)
    return (dest_all.astype(jnp.int32), meta_all.astype(jnp.int32))


def draw_tile_dest(key, part):
    return tile_layout(key)[0]


def draw_tile_meta(key, part):
    return tile_layout(key)[1]


def draw_qkv_weight(key, part):
    total_cols = 3 * HEADS * HD
    base_vals = jnp.clip(jax.random.normal(key, (D, total_cols), jnp.float32), -4.0, 4.0)
    return (base_vals * D ** (-0.5)).astype(jnp.bfloat16)


def draw_cotangent(key, part):
    row_frac = jnp.arange(ROWS).astype(jnp.float32) / ROWS
    noise = jnp.clip(jax.random.normal(key, (ROWS, HEADS * HD), jnp.float32), -4.0, 4.0)
    ramp = 1.0 + 2.0 * row_frac
    return (noise * ramp[:, None]).astype(jnp.bfloat16)


def block_levels(stream_key, extent, cuts, low, high):
    level = 1.0
    for dim, parts in cuts:
        draws = jax.random.uniform(jax.random.fold_in(jax.random.fold_in(stream_key, 6), dim), (parts,), jnp.float32, low / len(cuts), high / len(cuts))
        level = level * jnp.repeat(jnp.exp(draws), extent[dim] // parts).reshape((-1,) + (1,) * (len(extent) - 1 - dim))
    return level


def bell_draw(rng, shape, deviation, most, shards=(), held_as=jnp.bfloat16):
    array = jax.random.normal(rng, shape, jnp.float32) * deviation
    if len(shards) > 0:
        array = block_levels(rng, shape, shards, -0.22, 0.18) * array
    return jnp.clip(array, min=-most, max=most).astype(held_as)


def setup_inputs(seed: int = 0) -> dict:
    seeds = jax.random.split(jax.random.key(seed), 12)
    return {
        "tiles": bell_draw(seeds[0], (TILES_ALL, TILE_F, TILE_H, TILE_W, CH), 1.0, 6.0, ((0, 512),)),
        "tile_dest": draw_tile_dest(jax.random.fold_in(seeds[11], 71), 0),
        "tile_meta": draw_tile_meta(jax.random.fold_in(seeds[11], 71), 0),
        "space_weight": bell_draw(seeds[3], (9 * CH, CH), (9 * CH) ** -0.5, 0.15625),
        "time_weight": bell_draw(seeds[4], (3 * CH, CH), (3 * CH) ** -0.5, 0.25),
        "conv_bias": bell_draw(seeds[5], (CH,), 0.5, 3.0, (), jnp.float32),
        "latent_weight": bell_draw(seeds[6], (CH, LAT), CH ** -0.5, 0.4375),
        "embed_weight": bell_draw(seeds[7], (PATCH, D), PATCH ** -0.5, 0.75),
        "qkv_weight": draw_qkv_weight(jax.random.fold_in(seeds[11], 71), 0),
        "rope_freq": jnp.clip(jnp.exp(jax.random.uniform(seeds[9], (PAIRS,), jnp.float32, math.log(0.05), math.log(1.0))), 0.05, 1.0),
        "cotangent": draw_cotangent(jax.random.fold_in(seeds[11], 71), 0),
    }


score_floor = -1e+30

def encode(tile_block, space_weight, time_weight, conv_bias, latent_weight):
    tile_count, frames, height, width, channels = tile_block.shape
    padded = jnp.pad(tile_block, ((0, 0), (0, 0), (0, 1), (0, 1), (0, 0)))
    out_h = height // 2
    out_w = width // 2
    columns = []
    for row_off in range(3):
        for col_off in range(3):
            columns.append(padded[:, :, row_off:row_off + 2 * out_h - 1:2, col_off:col_off + 2 * out_w - 1:2, :])
    stacked = jnp.concatenate(columns, axis=-1).reshape(tile_count * frames * out_h * out_w, 9 * channels)
    spatial = jnp.dot(stacked, space_weight, preferred_element_type=jnp.float32).astype(jnp.bfloat16)
    spatial = spatial.reshape(tile_count, frames, out_h, out_w, channels)
    framed = jnp.pad(spatial, ((0, 0), (1, 0), (0, 0), (0, 0), (0, 0)))
    out_t = frames // 2
    time_cols = []
    for time_off in range(3):
        time_cols.append(framed[:, time_off:time_off + 2 * out_t - 1:2])
    time_stack = jnp.concatenate(time_cols, axis=-1).reshape(tile_count * out_t * out_h * out_w, 3 * channels)
    summed = jnp.dot(time_stack, time_weight, preferred_element_type=jnp.float32) + conv_bias
    features = jax.nn.silu(summed).astype(jnp.bfloat16)
    latents = jnp.dot(features, latent_weight, preferred_element_type=jnp.float32).astype(jnp.bfloat16)
    return latents.reshape(tile_count, out_t, out_h, out_w, latent_weight.shape[1])

def patchify(features):
    tile_count, out_t, out_h, out_w, channels = features.shape
    grid_blocks = features.reshape(tile_count, out_t, out_h // 2, 2, out_w // 2, 2, channels)
    grid_blocks = grid_blocks.transpose(0, 1, 2, 4, 3, 5, 6)
    return grid_blocks.reshape(tile_count * out_t * (out_h // 2) * (out_w // 2), 4 * channels)

def token_coords(tile_coords, out_t, patch_h, patch_w):
    places = tile_coords.shape[0]
    frame_idx = tile_coords[:, 0][:, None, None, None] * out_t + jnp.arange(out_t, dtype=jnp.int32)[None, :, None, None]
    row_idx = tile_coords[:, 1][:, None, None, None] * patch_h + jnp.arange(patch_h, dtype=jnp.int32)[None, None, :, None]
    col_idx = tile_coords[:, 2][:, None, None, None] * patch_w + jnp.arange(patch_w, dtype=jnp.int32)[None, None, None, :]
    grid_shape = (places, out_t, patch_h, patch_w)
    stacked = jnp.stack([jnp.broadcast_to(frame_idx, grid_shape), jnp.broadcast_to(row_idx, grid_shape), jnp.broadcast_to(col_idx, grid_shape)], axis=-1)
    return stacked.reshape(places * out_t * patch_h * patch_w, 3).astype(jnp.int32)

def rotate(values, coords, rope_freq):
    pair_count = rope_freq.shape[0]
    side_pairs = pair_count // 3
    time_pairs = pair_count - 2 * side_pairs
    pair_idx = jnp.arange(pair_count)[None, :]
    position = jnp.where(pair_idx < time_pairs, coords[:, 0:1], jnp.where(pair_idx < time_pairs + side_pairs, coords[:, 1:2], coords[:, 2:3]))
    angles = position.astype(rope_freq.dtype) * rope_freq[None, :]
    cosine = jnp.cos(angles)
    sine_part = jnp.sin(angles)
    left_half = values[:, :pair_count].astype(rope_freq.dtype)
    right_half = values[:, pair_count:].astype(rope_freq.dtype)
    turned = jnp.concatenate([left_half * cosine - right_half * sine_part, left_half * sine_part + right_half * cosine], axis=1)
    return turned.astype(jnp.bfloat16)

def attend(rope_freq, queries, key_rows, value_rows, query_coords, key_coords, query_live, key_live):
    query_rot = rotate(queries, query_coords, rope_freq)
    key_rot = rotate(key_rows, key_coords, rope_freq)
    scores = lax.dot_general(query_rot, key_rot, (((1,), (1,)), ((), ())), preferred_element_type=jnp.float32)
    scores = scores * queries.shape[1] ** (-0.5)
    scores = jnp.where(key_live[None, :] > 0, scores, score_floor)
    top_score = lax.stop_gradient(lax.optimization_barrier(jnp.max(scores, axis=1, keepdims=True)))
    weights = jnp.exp(scores - top_score)
    totals = lax.optimization_barrier(jnp.sum(weights, axis=1, keepdims=True))
    prob_rows = (weights / totals).astype(jnp.bfloat16)
    mixed_out = jnp.dot(prob_rows, value_rows, preferred_element_type=jnp.float32)
    return mixed_out * query_live[:, None].astype(mixed_out.dtype)

def head_pass(rope_freq, queries, key_rows, value_rows, cot_rows, query_coords, key_coords, query_live, key_live):

    def forward(freq_in):
        return attend(freq_in, queries, key_rows, value_rows, query_coords, key_coords, query_live, key_live)
    head_out, pullback = jax.vjp(forward, rope_freq)
    grads = pullback(cot_rows.astype(head_out.dtype))
    return (head_out, grads[0])

def reference(tiles, tile_dest, tile_meta, space_weight, time_weight, conv_bias, latent_weight, embed_weight, qkv_weight, rope_freq, cotangent):
    blocks = tiles.reshape((N_DP * N_SEQ, TILES_DEV) + tiles.shape[1:])

    def encode_block(tile_block):
        return encode(tile_block, space_weight, time_weight, conv_bias, latent_weight)
    features = lax.map(encode_block, blocks)
    features = features.reshape((TILES_ALL,) + features.shape[2:])
    tile_index = jnp.arange(TILES_ALL, dtype=jnp.int32)
    seq_index = tile_index // TILES_DEV % N_SEQ
    target_place = ((tile_dest * N_SEQ + seq_index) * OWN_MAX + tile_meta[:, 0]).astype(jnp.int32)
    place_total = N_DP * N_SEQ * OWN_MAX
    placed = jnp.zeros((place_total,) + features.shape[1:], features.dtype).at[target_place].set(features)
    tile_live = jnp.zeros((place_total,), jnp.int32).at[target_place].set(jnp.ones((TILES_ALL,), jnp.int32))
    tile_coords = jnp.zeros((place_total, 3), jnp.int32).at[target_place].set(tile_meta[:, 1:].astype(jnp.int32))
    out_t = features.shape[1]
    patch_h = features.shape[2] // 2
    patch_w = features.shape[3] // 2
    token_rows = patchify(placed)
    token_pos = token_coords(tile_coords, out_t, patch_h, patch_w)
    token_live = jnp.repeat(tile_live, out_t * patch_h * patch_w)
    span_width = qkv_weight.shape[1] // 3
    head_size = 2 * rope_freq.shape[0]
    head_count = span_width // head_size
    seq_rows = token_rows.reshape(N_DP, KEYS, token_rows.shape[1])
    seq_pos = token_pos.reshape(N_DP, KEYS, 3)
    seq_live = token_live.reshape(N_DP, KEYS)
    seq_cot = cotangent.reshape(N_DP, KEYS, span_width)

    def one_sequence(inputs):
        rows_in, pos_in, live_in, cot_in = inputs
        embedded = jnp.dot(rows_in, embed_weight, preferred_element_type=jnp.float32).astype(jnp.bfloat16)
        projected = jnp.dot(embedded, qkv_weight, preferred_element_type=jnp.float32).astype(jnp.bfloat16)
        outputs = []
        grad_total = jnp.zeros(rope_freq.shape, rope_freq.dtype)
        for head_idx in range(head_count):
            start_col = head_idx * head_size
            head_out, head_grad = head_pass(rope_freq, projected[:, start_col:start_col + head_size], projected[:, span_width + start_col:span_width + start_col + head_size], projected[:, 2 * span_width + start_col:2 * span_width + start_col + head_size], cot_in[:, start_col:start_col + head_size], pos_in, pos_in, live_in, live_in)
            outputs.append(head_out)
            grad_total = grad_total + head_grad
        return (jnp.concatenate(outputs, axis=1).astype(jnp.bfloat16), grad_total)
    attended, grads = lax.map(one_sequence, (seq_rows, seq_pos, seq_live, seq_cot))
    return (attended.reshape(ROWS, span_width), lax.optimization_barrier(jnp.sum(grads, axis=0)))
```

```python
import functools
import math

import jax
import jax.numpy as jnp
from jax import lax
from jax.experimental import pallas as pl
from jax.experimental.pallas import tpu as pltpu
from jax.sharding import PartitionSpec as P

F32 = jnp.float32
BF16 = jnp.bfloat16
META = 128
BIG = 1e30


def iota(shape, dim):
    return lax.broadcasted_iota(jnp.int32, shape, dim)


def dot(a, b):
    return jnp.dot(a, b, preferred_element_type=F32)


def dot_nt(a, b):
    return lax.dot_general(a, b, (((1,), (1,)), ((), ())), preferred_element_type=F32)


def encode_tiles(tiles_ref, space_ref, time_ref, bias_ref, latent_ref):
    held, frames, height, width, chans = tiles_ref.shape
    out_h = height // 2
    rows = held * width
    lat_wide = latent_ref.shape[1]
    total = jnp.zeros((rows, lat_wide), F32)
    lane = iota((rows, lat_wide), 1)
    col = iota((rows, lat_wide), 0) % width
    lane_h = 2 * (lane // 128) + (lane // 32) % 2
    lane_w = 2 * ((lane // 64) % 2) + (lane // 16) % 2
    at_col = 2 * lane_w == col
    edge = iota((1, width, chans), 1) < width - 2
    for h in range(out_h):
        shifted = [None, None, None]
        for row_off in range(3):
            src = 2 * h + row_off
            if src >= height:
                continue
            x = tiles_ref[:, :, src].reshape(held * frames * width, chans)
            for col_off in range(3):
                tap = (row_off * 3 + col_off) * chans
                part = dot(x, space_ref[tap : tap + chans, :])
                old = shifted[col_off]
                shifted[col_off] = part if old is None else old + part
        y0, y1, y2 = [y.reshape(held * frames, width, chans) for y in shifted]
        y1 = pltpu.roll(y1, width - 1, axis=1)
        y2 = jnp.where(edge, pltpu.roll(y2, width - 2, axis=1), 0.0)
        spatial = (y0 + y1 + y2).reshape(held, frames, width, chans)
        first = spatial[:, 0].reshape(rows, chans).astype(BF16)
        second = spatial[:, 1].reshape(rows, chans).astype(BF16)
        summed = dot(first, time_ref[chans : 2 * chans, :]) + dot(second, time_ref[2 * chans :, :])
        summed = summed + bias_ref[...]
        feats = (summed / (1.0 + jnp.exp(-summed))).astype(BF16)
        latents = dot(feats, latent_ref[...])
        total = total + jnp.where((lane_h == h) & at_col, latents, 0.0)
    return total.astype(BF16)


def encode_kernel(tiles_ref, space_ref, time_ref, bias_ref, latent_ref, slot8_ref, slot_ref, meta_ref, out_ref):
    latents = encode_tiles(tiles_ref, space_ref, time_ref, bias_ref, latent_ref)
    slots = out_ref.shape[0]
    rows = latents.shape[0]
    held = meta_ref.shape[0]
    pick = (iota((slots, rows), 0) == slot8_ref[...]).astype(F32).astype(BF16)
    out_ref[:, 0:256] = dot(pick, latents).astype(BF16)
    pick = (iota((slots, held), 0) == slot_ref[...]).astype(F32).astype(BF16)
    out_ref[:, 256:] = dot(pick, meta_ref[...]).astype(BF16)


def sincos(angle):
    turns = jnp.floor(angle * (0.5 / math.pi) + 0.5)
    r = angle - turns * 6.28125
    r = r - turns * (2.0 * math.pi - 6.28125)
    z = r * r
    s = jnp.full_like(z, -1.0 / math.factorial(15))
    for n in (13, 11, 9, 7, 5, 3, 1):
        s = s * z + (1.0 if n % 4 == 1 else -1.0) / math.factorial(n)
    c = jnp.full_like(z, 1.0 / math.factorial(16))
    for n in (14, 12, 10, 8, 6, 4, 2, 0):
        c = c * z + (1.0 if n % 4 == 0 else -1.0) / math.factorial(n)
    return s * r, c


def axis_masks(shape):
    pair = iota(shape, 1) % 64
    return pair < 22, (pair >= 22) & (pair < 43), pair >= 43


def swap_halves(u):
    lane = iota(u.shape, 1)
    turned = pltpu.roll(u, 64, axis=1)
    return jnp.where(lane < 64, -turned, turned)


def rotary_tables(freq):
    shape = (META, META)
    sub = iota(shape, 0)
    in_f, in_r, in_c = axis_masks(shape)
    step = jnp.where((sub == 1) & in_f, 1.0, 0.0)
    step = jnp.where(((sub == 2) & in_r) | ((sub == 3) & in_c), 2.0, step)
    rest = freq
    tables = []
    for _ in range(3):
        part = rest.astype(BF16).astype(F32)
        rest = rest - part
        tables.append((step * part).astype(BF16))
    return tables, step.astype(BF16)


def token_weights(ew_ref, freq, first):
    base = ew_ref[:, first : first + 128]
    shape = (8, 128)
    in_f, in_r, in_c = axis_masks(shape)
    blocks = []
    for tok in range(4):
        row_block, col_block = tok // 2, tok % 2
        offset = jnp.where(in_r, float(row_block), 0.0) + jnp.where(in_c, float(col_block), 0.0)
        s, c = sincos(jnp.broadcast_to(freq, shape) * offset)
        turned = base * c[0:1, :] + swap_halves(base) * s[0:1, :]
        blocks.append(jnp.concatenate([turned, swap_halves(turned)], axis=1))
    return jnp.concatenate(blocks, axis=0)


def attend_kernel(own_ref, all_ref, ew_ref, freq_ref, cot_ref, out_ref, grad_ref, keys_ref, vals_ref, score_ref):
    tiles = all_ref.shape[0]
    slots = own_ref.shape[0]
    tokens = 4 * slots
    keys = 4 * tiles
    freq = freq_ref[...]
    scale = 128.0 ** (-0.5)
    tables, step = rotary_tables(freq)

    def positions(meta):
        angle = dot(meta, tables[0]) + dot(meta, tables[1]) + dot(meta, tables[2])
        s, c = sincos(angle)
        return s, c, dot(meta, step)

    wk = token_weights(ew_ref, freq, 128)
    wq = token_weights(ew_ref, freq, 0)
    wv = ew_ref[:, 256:384]
    row4 = iota((256, 128), 0) // 64

    own = own_ref[...]
    pick8 = (iota((8, META), 0) == iota((8, META), 1)).astype(F32).astype(BF16)
    slot_meta = dot_nt(pick8, own[:, 256:])
    place_row = iota((tokens, slots), 0) // 4
    taken = (place_row.astype(F32) == slot_meta[0:1, :]) & (slot_meta[4:5, :] > 0.5)
    mine = dot(jnp.where(taken, 1.0, 0.0).astype(BF16), own)
    which = iota((tokens, 256), 0) % 4 == iota((tokens, 256), 1) // 64
    my_lat = jnp.where(which, mine[:, 0:256], 0.0).astype(BF16)
    my_meta = mine[:, 256:].astype(BF16)
    live = mine[:, 260:261]
    s, c, pos = positions(my_meta)
    u = dot(my_lat, wq.astype(BF16))
    q = u[:, 0:128] * c + u[:, 128:256] * s
    in_f, in_r, in_c = axis_masks((tokens, 128))
    tok = iota((tokens, 128), 0) % 4
    pos = pos + jnp.where(in_r, (tok // 2).astype(F32), 0.0) + jnp.where(in_c, (tok % 2).astype(F32), 0.0)
    lane4 = jnp.where(iota((tokens, META), 1) == 4, 1.0, 0.0).astype(BF16)
    q_ext = jnp.concatenate([lane4, (q * (scale * math.log2(math.e))).astype(BF16)], axis=1)

    block = min(256, tiles)
    for start in range(0, tiles, block):
        lat = all_ref[start : start + block, 0:256]
        meta = all_ref[start : start + block, 256:]
        s, c, kpos = positions(meta)
        dead = jnp.where(iota((block, META), 1) == 4, (meta.astype(F32) - 1.0) * BIG, 0.0).astype(BF16)
        in_f, in_r, in_c = axis_masks((1, 128))
        for tok in range(4):
            here = jnp.where(row4 == tok, jnp.concatenate([wv] * 4, axis=0), 0.0).astype(BF16)
            wide = jnp.where(iota((256, 256), 0) // 64 == tok, wk, 0.0).astype(BF16)
            u = dot(lat, wide)
            k = u[:, 0:128] * c + u[:, 128:256] * s
            offset = jnp.where(in_r, float(tok // 2), 0.0) + jnp.where(in_c, float(tok % 2), 0.0)
            at = tok * tiles + start
            keys_ref[at : at + block, 0:128] = dead
            keys_ref[at : at + block, 128:256] = k.astype(BF16)
            keys_ref[at : at + block, 256:384] = (k * (kpos + offset)).astype(BF16)
            vals_ref[at : at + block, :] = dot(lat, here).astype(BF16)

    chunk = 512
    starts = range(0, keys, chunk)
    top = jnp.full((tokens, chunk), -jnp.inf, F32)
    for at in starts:
        scores = dot_nt(q_ext, keys_ref[at : at + chunk, 0:256])
        score_ref[:, at : at + chunk] = scores
        top = jnp.maximum(top, scores)
    top = jnp.max(top, axis=1, keepdims=True)
    sums = jnp.zeros((tokens, chunk), F32)
    mixed = jnp.zeros((tokens, 128), F32)
    for at in starts:
        weights = jnp.exp2(score_ref[:, at : at + chunk] - top)
        score_ref[:, at : at + chunk] = weights
        sums = sums + weights
        mixed = mixed + dot(weights.astype(BF16), vals_ref[at : at + chunk, :])
    inv = 1.0 / jnp.sum(sums, axis=1, keepdims=True)
    mixed = mixed * inv
    out_ref[...] = (mixed * live).astype(BF16)
    cot = cot_ref[...]
    mean = jnp.sum(cot.astype(F32) * mixed, axis=1, keepdims=True)
    back = jnp.zeros((tokens, 256), F32)
    for at in starts:
        dprob = dot_nt(cot, vals_ref[at : at + chunk, :])
        dscore = score_ref[:, at : at + chunk] * (dprob - mean)
        back = back + dot(dscore.astype(BF16), keys_ref[at : at + chunk, 128:384])
    row_fac = inv * live * scale
    g = pltpu.roll(back[:, 0:128], 64, axis=1)
    gp = pltpu.roll(back[:, 128:256], 64, axis=1)
    terms = q * (pos * g - gp) * row_fac
    line = jnp.sum(terms, axis=0, keepdims=True)
    lane = iota((1, 128), 1)
    other = pltpu.roll(line, 64, axis=1)
    grad_ref[...] = jnp.where(lane < 64, line - other, other - line)


def per_device(
    tiles,
    tile_dest,
    tile_meta,
    space_weight,
    time_weight,
    conv_bias,
    latent_weight,
    embed_weight,
    qkv_weight,
    rope_freq,
    cotangent,
):
    loaders = lax.axis_size("dp")
    held = tiles.shape[0]
    slots = 2 * held
    capacity = slots // loaders
    order = jnp.arange(held, dtype=jnp.int32)
    same = (tile_dest[:, None] == tile_dest[None, :]) & (order[:, None] < order[None, :])
    rank = jnp.sum(same.astype(jnp.int32), axis=0)
    slot = tile_dest * capacity + rank
    meta = jnp.concatenate([tile_meta, jnp.ones((held, 1), jnp.int32)], axis=1)
    meta = jnp.pad(meta, ((0, 0), (0, META - 5))).astype(BF16)
    outgoing = pl.pallas_call(
        encode_kernel,
        out_shape=jax.ShapeDtypeStruct((slots, 256 + META), BF16),
        compiler_params=pltpu.CompilerParams(vmem_limit_bytes=48 << 20),
    )(
        tiles,
        space_weight,
        time_weight,
        conv_bias[None, :],
        jnp.tile(latent_weight, (1, 16)),
        jnp.repeat(slot, tiles.shape[3])[None, :],
        slot[None, :],
        meta,
    )
    shard = qkv_weight.shape[0]
    mine = lax.dynamic_slice_in_dim(embed_weight, lax.axis_index("seq") * shard, shard, 1)
    folded = lax.psum(jnp.dot(mine, qkv_weight, preferred_element_type=F32), "seq")
    arrived = lax.all_to_all(
        outgoing.reshape(loaders, capacity, -1), "dp", split_axis=0, concat_axis=0, tiled=True
    ).reshape(slots, -1)
    gathered = lax.all_gather(arrived, "seq", axis=0, tiled=True)
    tokens = 4 * slots
    keys = 4 * gathered.shape[0]
    attended, grad = pl.pallas_call(
        attend_kernel,
        out_shape=(
            jax.ShapeDtypeStruct((tokens, 128), BF16),
            jax.ShapeDtypeStruct((1, 128), F32),
        ),
        scratch_shapes=[
            pltpu.VMEM((keys, 384), BF16),
            pltpu.VMEM((keys, 128), BF16),
            pltpu.VMEM((tokens, keys), F32),
        ],
        compiler_params=pltpu.CompilerParams(vmem_limit_bytes=48 << 20),
    )(arrived, gathered, folded, jnp.tile(rope_freq, 2)[None, :], cotangent)
    freq_grad = lax.psum(grad[0, :64], ("dp", "seq"))
    return attended, freq_grad


def solution(mesh):
    both = ("dp", "seq")
    specs = (
        P(both, None, None, None, None),
        P(both),
        P(both, None),
        P(),
        P(),
        P(),
        P(),
        P(),
        P("seq", None),
        P(),
        P(both, None),
    )
    return jax.shard_map(
        per_device,
        mesh=mesh,
        in_specs=specs,
        out_specs=(P(both, None), P()),
        check_vma=False,
    )
```

```python
import math

import jax
import jax.numpy as jnp
from jax import lax
from jax.experimental import pallas as pl
from jax.experimental.pallas import tpu as pltpu
from jax.sharding import PartitionSpec as P

F32 = jnp.float32
BF16 = jnp.bfloat16
MESH = pl.DeviceIdType.MESH
META = 128
BIG = 1e30
UNITS = 24
FIELDS = 16


def iota(shape, dim):
    return lax.broadcasted_iota(jnp.int32, shape, dim)


def dot(a, b):
    return jnp.dot(a, b, preferred_element_type=F32)


def dot_nt(a, b):
    return lax.dot_general(a, b, (((1,), (1,)), ((), ())), preferred_element_type=F32)


def dot_tn(a, b):
    return lax.dot_general(a, b, (((0,), (0,)), ((), ())), preferred_element_type=F32)


def one_hot(cond):
    return jnp.where(cond, 1.0, 0.0).astype(BF16)


def encode_rows(h, tiles_ref, space_ref, time_ref, bias_ref, latent_ref):
    held, frames, height, width, chans = tiles_ref.shape
    rows = held * width
    lat_wide = latent_ref.shape[1]
    shifted = [None, None, None]
    for row_off in range(3):
        src = 2 * h + row_off
        if src >= height:
            continue
        x = tiles_ref[:, :, src].reshape(held * frames * width, chans)
        for col_off in range(3):
            tap = (row_off * 3 + col_off) * chans
            part = dot(x, space_ref[tap : tap + chans, :])
            old = shifted[col_off]
            shifted[col_off] = part if old is None else old + part
    y0, y1, y2 = [y.reshape(held * frames, width, chans) for y in shifted]
    y1 = pltpu.roll(y1, width - 1, axis=1)
    edge = iota((1, width, chans), 1) < width - 2
    y2 = jnp.where(edge, pltpu.roll(y2, width - 2, axis=1), 0.0)
    spatial = (y0 + y1 + y2).reshape(held, frames, width, chans)
    first = spatial[:, 0].reshape(rows, chans).astype(BF16)
    second = spatial[:, 1].reshape(rows, chans).astype(BF16)
    summed = dot(first, time_ref[chans : 2 * chans, :]) + dot(second, time_ref[2 * chans :, :])
    summed = summed + bias_ref[...]
    feats = (summed / (1.0 + jnp.exp(-summed))).astype(BF16)
    lane = iota((rows, lat_wide), 1)
    lane_h = 2 * (lane // 128) + (lane // 32) % 2
    lane_w = 2 * ((lane // 64) % 2) + (lane // 16) % 2
    keep = (lane_h == h) & (2 * lane_w == iota((rows, lat_wide), 0) % width)
    return jnp.where(keep, dot(feats, latent_ref[...]), 0.0)


def pack_messages(latents, slot8_ref, slot_ref, meta_ref, out_ref):
    owners = out_ref.shape[0]
    rows = latents.shape[0]
    held = meta_ref.shape[0]
    latents = latents.astype(BF16)
    shape = (8 * owners, rows)
    sub = iota(shape, 0) % 8
    hit = (2 * (iota(shape, 0) // 8) + sub // 2 == slot8_ref[...]) & (sub < 4)
    packed = dot(one_hot(hit & (sub % 2 == 0)), latents[:, 0:128])
    packed = packed + dot(one_hot(hit & (sub % 2 == 1)), latents[:, 128:256])
    shape = (8 * owners, held)
    hit = (iota(shape, 0) // 8 == slot_ref[...] // 2) & (iota(shape, 0) % 8 == 4)
    packed = packed + dot(one_hot(hit), meta_ref[...])
    out_ref[...] = packed.astype(BF16).reshape(owners, 8, 128)


def unpack_messages(arrived, block_ref, mine):
    loaders = arrived.shape[0]
    slots = 2 * loaders
    flat = arrived.reshape(8 * loaders, 128)
    shape = (slots, 8 * loaders)
    base = 8 * (iota(shape, 0) // 2) + 2 * (iota(shape, 0) % 2)
    block_ref[mine, 0:slots, 0:128] = dot(one_hot(iota(shape, 1) == base), flat).astype(BF16)
    block_ref[mine, 0:slots, 128:256] = dot(one_hot(iota(shape, 1) == base + 1), flat).astype(BF16)
    both = dot(one_hot(iota(shape, 1) == 8 * (iota(shape, 0) // 2) + 4), flat)
    odd = iota((slots, META), 0) % 2 == 1
    fields = jnp.where(odd, pltpu.roll(both, META - 8, axis=1), both)
    pick = one_hot((iota((FIELDS, META), 0) == iota((FIELDS, META), 1)) & (iota((FIELDS, META), 1) < 8))
    turned = dot_nt(pick, fields.astype(BF16)).astype(BF16)
    wide = jnp.concatenate([turned, jnp.zeros((FIELDS, 256 - slots), BF16)], axis=1)
    block_ref[mine, slots : slots + FIELDS, :] = wide


def sincos(angle):
    turns = jnp.floor(angle * (0.5 / math.pi) + 0.5)
    r = angle - turns * 6.28125
    r = r - turns * (2.0 * math.pi - 6.28125)
    z = r * r
    s = jnp.full_like(z, -1.0 / math.factorial(15))
    for n in (13, 11, 9, 7, 5, 3, 1):
        s = s * z + (1.0 if n % 4 == 1 else -1.0) / math.factorial(n)
    c = jnp.full_like(z, 1.0 / math.factorial(16))
    for n in (14, 12, 10, 8, 6, 4, 2, 0):
        c = c * z + (1.0 if n % 4 == 0 else -1.0) / math.factorial(n)
    return s * r, c


def axis_masks(shape):
    pair = iota(shape, 1) % 64
    return pair < 22, (pair >= 22) & (pair < 43), pair >= 43


def swap_halves(u):
    lane = iota(u.shape, 1)
    turned = pltpu.roll(u, 64, axis=1)
    return jnp.where(lane < 64, -turned, turned)


def rotary_tables(freq):
    shape = (FIELDS, META)
    sub = iota(shape, 0)
    in_f, in_r, in_c = axis_masks(shape)
    step = jnp.where((sub == 1) & in_f, 1.0, 0.0)
    step = jnp.where(((sub == 2) & in_r) | ((sub == 3) & in_c), 2.0, step)
    rest = jnp.broadcast_to(freq, shape)
    tables = []
    for _ in range(3):
        part = rest.astype(BF16).astype(F32)
        rest = rest - part
        tables.append((step * part).astype(BF16))
    return jnp.concatenate(tables + [step.astype(BF16)], axis=1)


def token_weights(ew_ref, freq, first):
    base = ew_ref[:, first : first + 128]
    shape = (8, 128)
    in_f, in_r, in_c = axis_masks(shape)
    blocks = []
    for tok in range(4):
        offset = jnp.where(in_r, float(tok // 2), 0.0) + jnp.where(in_c, float(tok % 2), 0.0)
        s, c = sincos(jnp.broadcast_to(freq, shape) * offset)
        turned = base * c[0:1, :] + swap_halves(base) * s[0:1, :]
        blocks.append(jnp.concatenate([turned, swap_halves(turned)], axis=1))
    return jnp.concatenate(blocks, axis=0).astype(BF16)


def from_fields(fields, tables):
    wide = dot_tn(fields, tables)
    angle = wide[:, 0:128] + wide[:, 128:256] + wide[:, 256:384]
    s, c = sincos(angle)
    return s, c, wide[:, 384:512]


def project_keys(lat, fields, tables, wk, wv, keys_ref, vals_ref, at):
    slots = lat.shape[0]
    tokens = 4 * slots
    s, c, pos = from_fields(fields, tables)
    which = iota((tokens, 256), 0) // slots == iota((tokens, 256), 1) // 64
    spread = jnp.where(which, jnp.concatenate([lat.astype(F32)] * 4, axis=0), 0.0).astype(BF16)
    u = dot(spread, wk)
    tok = iota((tokens, 128), 0) // slots
    in_f, in_r, in_c = axis_masks((tokens, 128))
    shift = jnp.where(in_r & (tok >= 2), 1.0, 0.0) + jnp.where(in_c & (tok % 2 == 1), 1.0, 0.0)
    k = u[:, 0:128] * jnp.concatenate([c] * 4, axis=0) + u[:, 128:256] * jnp.concatenate([s] * 4, axis=0)
    pick = one_hot((iota((FIELDS, META), 0) == 4) & (iota((FIELDS, META), 1) == 0))
    dead = jnp.where(iota((slots, META), 1) == 0, (dot_tn(fields, pick) - 1.0) * BIG, 0.0).astype(BF16)
    keys_ref[pl.ds(at, tokens), 0:128] = jnp.concatenate([dead] * 4, axis=0)
    keys_ref[pl.ds(at, tokens), 128:256] = k.astype(BF16)
    keys_ref[pl.ds(at, tokens), 256:384] = (k * (jnp.concatenate([pos] * 4, axis=0) + shift)).astype(BF16)
    vals_ref[pl.ds(at, tokens), :] = dot(spread, wv).astype(BF16)


def project_queries(lat, fields, tables, wq):
    slots = lat.shape[0]
    tokens = 4 * slots
    taken = (iota((tokens, slots), 0) // 4).astype(F32) == fields[0:1, :].astype(F32)
    chosen = one_hot(taken & (fields[4:5, :].astype(F32) > 0.5))
    which = iota((tokens, 256), 0) % 4 == iota((tokens, 256), 1) // 64
    my_lat = jnp.where(which, dot(chosen, lat), 0.0).astype(BF16)
    my_fields = dot_nt(fields, chosen).astype(BF16)
    s, c, pos = from_fields(my_fields, tables)
    pick = one_hot(iota((FIELDS, META), 0) == 4)
    live = dot_tn(my_fields, pick)
    u = dot(my_lat, wq)
    q = u[:, 0:128] * c + u[:, 128:256] * s
    in_f, in_r, in_c = axis_masks((tokens, 128))
    tok = iota((tokens, 128), 0) % 4
    pos = pos + jnp.where(in_r & (tok >= 2), 1.0, 0.0) + jnp.where(in_c & (tok % 2 == 1), 1.0, 0.0)
    lane0 = one_hot(iota((tokens, META), 1) == 0)
    scale = 128.0 ** (-0.5) * math.log2(math.e)
    q_ext = jnp.concatenate([lane0, (q * scale).astype(BF16)], axis=1)
    return q, q_ext, pos, live


def finish_attention(q, q_ext, pos, live, top, cot_ref, out_ref, keys_ref, vals_ref, score_ref):
    tokens = q.shape[0]
    keys = keys_ref.shape[0]
    chunk = min(512, keys)
    starts = range(0, keys, chunk)
    top = jnp.max(top, axis=1, keepdims=True)
    sums = jnp.zeros((tokens, chunk), F32)
    mixed = jnp.zeros((tokens, 128), F32)
    for at in starts:
        weights = jnp.exp2(score_ref[:, at : at + chunk] - top)
        score_ref[:, at : at + chunk] = weights
        sums = sums + weights
        mixed = mixed + dot(weights.astype(BF16), vals_ref[at : at + chunk, :])
    inv = 1.0 / jnp.sum(sums, axis=1, keepdims=True)
    mixed = mixed * inv
    out_ref[...] = (mixed * live).astype(BF16)
    cot = cot_ref[...]
    mean = jnp.sum(cot.astype(F32) * mixed, axis=1, keepdims=True)
    back = jnp.zeros((tokens, 256), F32)
    for at in starts:
        dprob = dot_nt(cot, vals_ref[at : at + chunk, :])
        dscore = score_ref[:, at : at + chunk] * (dprob - mean)
        back = back + dot(dscore.astype(BF16), keys_ref[at : at + chunk, 128:384])
    g = pltpu.roll(back[:, 0:128], 64, axis=1)
    gp = pltpu.roll(back[:, 128:256], 64, axis=1)
    terms = q * (pos * g - gp) * (inv * 128.0 ** (-0.5) * live)
    line = jnp.sum(terms, axis=0, keepdims=True)
    other = pltpu.roll(line, 64, axis=1)
    return jnp.where(iota((1, 128), 1) < 64, line - other, other - line)


def greet():
    me_dp, me_seq = lax.axis_index("dp"), lax.axis_index("seq")
    n_dp, n_seq = lax.axis_size("dp"), lax.axis_size("seq")
    barrier = pltpu.get_barrier_semaphore()

    def to_dp(i, _):
        peer = lax.rem(me_dp + i, n_dp)
        pl.semaphore_signal(barrier, inc=1, device_id=(peer, me_seq), device_id_type=MESH)
        return 0

    def to_seq(i, _):
        peer = lax.rem(me_seq + i, n_seq)
        pl.semaphore_signal(barrier, inc=1, device_id=(me_dp, peer), device_id_type=MESH)
        return 0

    lax.fori_loop(1, n_dp, to_dp, 0)
    lax.fori_loop(1, n_seq, to_seq, 0)
    return barrier, n_dp + n_seq - 2


def spread(axis, src_of, dst_ref, send_sem, recv_sem):
    me_dp, me_seq = lax.axis_index("dp"), lax.axis_index("seq")
    n = lax.axis_size(axis)
    me = lax.axis_index(axis)

    def copy(peer, slot):
        where = (peer, me_seq) if axis == "dp" else (me_dp, peer)
        return pltpu.make_async_remote_copy(
            src_ref=src_of(peer),
            dst_ref=dst_ref.at[slot],
            send_sem=send_sem.at[peer],
            recv_sem=recv_sem.at[slot],
            device_id=where,
            device_id_type=MESH,
        )

    def each(act):
        def body(i, _):
            act(lax.rem(me + i, n))
            return 0

        lax.fori_loop(1, n, body, 0)

    def start():
        each(lambda peer: copy(peer, me).start())

    def wait_recv():
        each(lambda peer: copy(peer, peer).wait_recv())

    def wait_send():
        each(lambda peer: copy(peer, me).wait_send())

    return start, wait_recv, wait_send


def fold_partial(embed_ref, qkv_ref, unit, window, sem):
    shard = qkv_ref.shape[0]
    wide = window.shape[1]
    me_seq = lax.axis_index("seq")
    first = (me_seq * shard) // 128 * 128
    rows = pl.ds(pl.multiple_of(8 * (unit // 3), 8), 8)
    load = pltpu.make_async_copy(embed_ref.at[rows, pl.ds(pl.multiple_of(first, 128), wide)], window, sem)
    load.start()
    load.wait()
    part = window[...].astype(F32)
    if wide != shard:
        part = jnp.where(me_seq % 2 == 1, pltpu.roll(part, wide - 64, axis=1), part)
    cols = pl.ds(pl.multiple_of(128 * (unit % 3), 128), 128)
    return dot(part[:, 0:shard].astype(BF16), qkv_ref[:, cols])


def gather_kernel(
    out_ref,
    embed_ref,
    qkv_ref,
    block_ref,
    ew_ref,
    window,
    load_sem,
    parts,
    unit_buf,
    unit_all,
    arrived,
    part_send,
    part_recv,
    unit_send,
    unit_recv,
    msg_send,
    msg_recv,
    ring_send,
    ring_recv,
):
    me_dp, me_seq = lax.axis_index("dp"), lax.axis_index("seq")
    n_dp, n_seq = lax.axis_size("dp"), lax.axis_size("seq")
    barrier, count = greet()
    per = parts.shape[1]
    for j in range(per):
        unit = lax.rem(me_dp * per + j, UNITS)
        parts[me_seq, j] = fold_partial(embed_ref, qkv_ref, unit, window, load_sem)
    pl.semaphore_wait(barrier, count)

    start_parts, recv_parts, sent_parts = spread("seq", lambda peer: parts.at[me_seq], parts, part_send, part_recv)
    start_msgs, recv_msgs, sent_msgs = spread("dp", lambda peer: out_ref.at[peer], arrived, msg_send, msg_recv)
    start_units, recv_units, sent_units = spread("dp", lambda peer: unit_buf, unit_all, unit_send, unit_recv)

    start_msgs()
    start_parts()
    arrived[me_dp] = out_ref[me_dp]
    recv_msgs()
    unpack_messages(arrived[...], block_ref, me_seq)

    right, left = lax.rem(me_seq + 1, n_seq), lax.rem(me_seq + n_seq - 1, n_seq)

    def hop(owner, to, way):
        return pltpu.make_async_remote_copy(
            src_ref=block_ref.at[owner],
            dst_ref=block_ref.at[owner],
            send_sem=ring_send.at[way, owner],
            recv_sem=ring_recv.at[owner],
            device_id=(me_dp, to),
            device_id_type=MESH,
        )

    far_right, far_left = n_seq // 2, (n_seq - 1) // 2
    hop(me_seq, right, 0).start()
    if far_left:
        hop(me_seq, left, 1).start()

    recv_parts()
    unit_buf[...] = jnp.sum(parts[...], axis=0)
    unit_all[me_dp] = unit_buf[...]
    start_units()

    def step(t, _):
        owner = lax.rem(me_seq + n_seq - t, n_seq)
        hop(owner, right, 0).wait_recv()

        @pl.when(t < far_right)
        def _():
            hop(owner, right, 0).start()

        @pl.when(t <= far_left)
        def _():
            owner = lax.rem(me_seq + t, n_seq)
            hop(owner, left, 1).wait_recv()

            @pl.when(t < far_left)
            def _():
                hop(owner, left, 1).start()

        return 0

    lax.fori_loop(1, far_right + 1, step, 0)
    recv_units()
    for unit in range(UNITS):
        ew_ref[8 * (unit // 3) : 8 * (unit // 3) + 8, 128 * (unit % 3) : 128 * (unit % 3) + 128] = unit_all[unit // per, unit % per]

    def drain(t, _):
        hop(lax.rem(me_seq + n_seq - t, n_seq), right, 0).wait_send()

        @pl.when(t < far_left)
        def _():
            hop(lax.rem(me_seq + t, n_seq), left, 1).wait_send()

        return 0

    lax.fori_loop(0, far_right, drain, 0)
    sent_msgs()
    sent_parts()
    sent_units()


def attend_kernel(block_ref, ew_ref, freq_ref, cot_ref, out_ref, grad_ref, keys_ref, vals_ref, score_ref):
    n_seq, rows, _ = block_ref.shape
    slots = rows - FIELDS
    tokens = 4 * slots
    freq = freq_ref[...]
    tables = rotary_tables(freq)
    me_seq = lax.axis_index("seq")
    wq = token_weights(ew_ref, freq, 0)
    wk = token_weights(ew_ref, freq, 128)
    wv = jnp.concatenate([ew_ref[:, 256:384]] * 4, axis=0).astype(BF16)
    mine = block_ref.at[me_seq]
    q, q_ext, pos, live = project_queries(mine[0:slots, :], mine[slots:, 0:slots], tables, wq)

    def step(i, top):
        at = pl.multiple_of(i * tokens, tokens)
        block = block_ref.at[i]
        project_keys(block[0:slots, :], block[slots:, 0:slots], tables, wk, wv, keys_ref, vals_ref, at)
        scores = dot_nt(q_ext, keys_ref[pl.ds(at, tokens), 0:256])
        score_ref[:, pl.ds(at, tokens)] = scores
        return jnp.maximum(top, scores)

    top = lax.fori_loop(0, n_seq, step, jnp.full((tokens, tokens), -jnp.inf, F32))
    grad_ref[...] = finish_attention(q, q_ext, pos, live, top, cot_ref, out_ref, keys_ref, vals_ref, score_ref)


def sum_kernel(line_ref, out_ref, by_seq, by_dp, mid, seq_send, seq_recv, dp_send, dp_recv):
    me_dp, me_seq = lax.axis_index("dp"), lax.axis_index("seq")
    barrier, count = greet()
    by_seq[me_seq] = line_ref[...]
    pl.semaphore_wait(barrier, count)
    start, recv, sent = spread("seq", lambda peer: line_ref, by_seq, seq_send, seq_recv)
    start()
    recv()
    mid[...] = jnp.sum(by_seq[...], axis=0)
    by_dp[me_dp] = mid[...]
    start2, recv2, sent2 = spread("dp", lambda peer: mid, by_dp, dp_send, dp_recv)
    start2()
    recv2()
    out_ref[...] = jnp.sum(by_dp[...], axis=0)
    sent()
    sent2()


def per_device(
    tiles,
    tile_dest,
    tile_meta,
    space_weight,
    time_weight,
    conv_bias,
    latent_weight,
    embed_weight,
    qkv_weight,
    rope_freq,
    cotangent,
):
    n_dp, n_seq = lax.axis_size("dp"), lax.axis_size("seq")
    held = tiles.shape[0]
    slots = 2 * n_dp
    tokens = 4 * slots
    keys = tokens * n_seq
    per = -(-UNITS // n_dp)
    order = jnp.arange(held, dtype=jnp.int32)
    same = (tile_dest[:, None] == tile_dest[None, :]) & (order[:, None] < order[None, :])
    rank = jnp.sum(same.astype(jnp.int32), axis=0)
    slot = tile_dest * 2 + rank
    meta = jnp.concatenate([tile_meta, jnp.ones((held, 1), jnp.int32)], axis=1)
    meta = jnp.tile(jnp.pad(meta, ((0, 0), (0, 3))), (1, META // 8))
    meta = jnp.where(jnp.arange(META)[None, :] // 8 == rank[:, None], meta, 0).astype(BF16)

    def encode_kernel(tiles_ref, space_ref, time_ref, bias_ref, latent_ref, slot8_ref, slot_ref, meta_ref, out_ref):
        total = None
        for h in range(tiles_ref.shape[2] // 2):
            part = encode_rows(h, tiles_ref, space_ref, time_ref, bias_ref, latent_ref)
            total = part if total is None else total + part
        pack_messages(total, slot8_ref, slot_ref, meta_ref, out_ref)

    outgoing = pl.pallas_call(
        encode_kernel,
        out_shape=jax.ShapeDtypeStruct((n_dp, 8, 128), BF16),
        compiler_params=pltpu.CompilerParams(vmem_limit_bytes=48 << 20),
    )(
        tiles,
        space_weight,
        time_weight,
        conv_bias[None, :],
        jnp.tile(latent_weight, (1, 16)),
        jnp.repeat(slot, tiles.shape[3])[None, :],
        slot[None, :],
        meta,
    )
    shard = qkv_weight.shape[0]
    vmem = pl.BlockSpec(memory_space=pltpu.VMEM)
    dma = pltpu.SemaphoreType.DMA
    blocks, folded = pl.pallas_call(
        gather_kernel,
        out_shape=(
            jax.ShapeDtypeStruct((n_seq, slots + FIELDS, 256), BF16),
            jax.ShapeDtypeStruct((64, 384), F32),
        ),
        in_specs=[vmem, pl.BlockSpec(memory_space=pl.ANY), vmem],
        out_specs=(vmem, vmem),
        scratch_shapes=[
            pltpu.VMEM((8, -(-shard // 128) * 128), BF16),
            dma(()),
            pltpu.VMEM((n_seq, per, 8, 128), F32),
            pltpu.VMEM((per, 8, 128), F32),
            pltpu.VMEM((n_dp, per, 8, 128), F32),
            pltpu.VMEM((n_dp, 8, 128), BF16),
            dma((n_seq,)),
            dma((n_seq,)),
            dma((n_dp,)),
            dma((n_dp,)),
            dma((n_dp,)),
            dma((n_dp,)),
            dma((2, n_seq)),
            dma((n_seq,)),
        ],
        compiler_params=pltpu.CompilerParams(
            vmem_limit_bytes=32 << 20, collective_id=0, has_side_effects=True
        ),
    )(outgoing, embed_weight, qkv_weight)
    attended, grad = pl.pallas_call(
        attend_kernel,
        out_shape=(
            jax.ShapeDtypeStruct((tokens, 128), BF16),
            jax.ShapeDtypeStruct((1, 128), F32),
        ),
        scratch_shapes=[
            pltpu.VMEM((keys, 384), BF16),
            pltpu.VMEM((keys, 128), BF16),
            pltpu.VMEM((tokens, keys), F32),
        ],
        compiler_params=pltpu.CompilerParams(vmem_limit_bytes=48 << 20),
    )(blocks, folded, jnp.tile(rope_freq, 2)[None, :], cotangent)
    summed = pl.pallas_call(
        sum_kernel,
        out_shape=jax.ShapeDtypeStruct((1, 128), F32),
        in_specs=[vmem],
        out_specs=vmem,
        scratch_shapes=[
            pltpu.VMEM((n_seq, 1, 128), F32),
            pltpu.VMEM((n_dp, 1, 128), F32),
            pltpu.VMEM((1, 128), F32),
            dma((n_seq,)),
            dma((n_seq,)),
            dma((n_dp,)),
            dma((n_dp,)),
        ],
        compiler_params=pltpu.CompilerParams(
            vmem_limit_bytes=32 << 20, collective_id=1, has_side_effects=True
        ),
    )(grad)
    return attended, summed[0, :64]


def solution(mesh):
    both = ("dp", "seq")
    specs = (
        P(both, None, None, None, None),
        P(both),
        P(both, None),
        P(),
        P(),
        P(),
        P(),
        P(),
        P("seq", None),
        P(),
        P(both, None),
    )
    return jax.shard_map(
        per_device,
        mesh=mesh,
        in_specs=specs,
        out_specs=(P(both, None), P()),
        check_vma=False,
    )
```

```python
import math

import jax
import jax.numpy as jnp
from jax import lax
from jax.experimental import pallas as pl
from jax.experimental.pallas import tpu as pltpu
from jax.sharding import PartitionSpec as P

F32 = jnp.float32
BF16 = jnp.bfloat16
MESH = pl.DeviceIdType.MESH
META = 128
BIG = 1e30
UNITS = 24
FIELDS = 8


def iota(shape, dim):
    return lax.broadcasted_iota(jnp.int32, shape, dim)


def dot(a, b):
    return jnp.dot(a, b, preferred_element_type=F32)


def dot_nt(a, b):
    return lax.dot_general(a, b, (((1,), (1,)), ((), ())), preferred_element_type=F32)


def dot_tn(a, b):
    return lax.dot_general(a, b, (((0,), (0,)), ((), ())), preferred_element_type=F32)


def one_hot(cond):
    return jnp.where(cond, 1.0, 0.0).astype(BF16)


def place_tiles(dest_ref, meta_ref, owners):
    held = dest_ref.shape[1]
    square = (held, held)
    row = jnp.broadcast_to(dest_ref[...].astype(F32), square)
    first, second = iota(square, 0), iota(square, 1)
    col = jnp.sum(jnp.where(first == second, row, 0.0), axis=1, keepdims=True)
    same = jnp.where(col == row, 1.0, 0.0)
    rank_row = jnp.sum(jnp.where(first < second, same, 0.0), axis=0, keepdims=True)
    rank_col = jnp.sum(jnp.where(second < first, same, 0.0), axis=1, keepdims=True)
    slot_row = 2.0 * row[0:1, :] + rank_row
    shape = (8, held)
    fields = jnp.concatenate([meta_ref[...].astype(F32), jnp.ones((4, held), F32)], axis=0)
    fields = jnp.where(iota(shape, 0) < 5, fields, 0.0).astype(BF16)
    pick = one_hot(iota((8, META), 0) == iota((8, META), 1) % 8)
    lanes = dot_tn(fields, pick)
    ranked = jnp.where((iota((held, META), 1) // 8).astype(F32) == rank_col, lanes, 0.0).astype(BF16)
    return slot_row, ranked


def encode_rows(h, tiles_ref, space_ref, time_ref, bias, latent):
    held, frames, height, width, chans = tiles_ref.shape
    rows = held * width
    lat_wide = latent.shape[0]
    shifted = [None, None, None]
    for row_off in range(3):
        src = 2 * h + row_off
        if src >= height:
            continue
        x = tiles_ref[:, :, src].reshape(held * frames * width, chans)
        for col_off in range(3):
            part = dot(x, space_ref[row_off * 3 + col_off])
            old = shifted[col_off]
            shifted[col_off] = part if old is None else old + part
    y0, y1, y2 = [y.reshape(held * frames, width, chans) for y in shifted]
    y1 = pltpu.roll(y1, width - 1, axis=1)
    edge = iota((1, width, chans), 1) < width - 2
    y2 = jnp.where(edge, pltpu.roll(y2, width - 2, axis=1), 0.0)
    spatial = (y0 + y1 + y2).reshape(held, frames, width, chans)
    first = spatial[:, 0].reshape(rows, chans).astype(BF16)
    second = spatial[:, 1].reshape(rows, chans).astype(BF16)
    summed = dot(first, time_ref[0]) + dot(second, time_ref[1]) + bias
    feats = (summed / (1.0 + jnp.exp(-summed))).astype(BF16)
    lane = iota((rows, lat_wide), 1)
    lane_h = 2 * (lane // 128) + (lane // 32) % 2
    lane_w = 2 * ((lane // 64) % 2) + (lane // 16) % 2
    keep = (lane_h == h) & (2 * lane_w == iota((rows, lat_wide), 0) % width)
    return jnp.where(keep, dot_nt(feats, latent), 0.0)


def pack_messages(latents, slot_row, ranked, width, out_ref):
    owners = out_ref.shape[0]
    rows = latents.shape[0]
    held = ranked.shape[0]
    latents = latents.astype(BF16)
    shape = (8 * owners, held)
    sub = iota(shape, 0) % 8
    mine = (2 * (iota(shape, 0) // 8) + sub // 2).astype(F32) == slot_row
    hit = one_hot(mine & (sub < 4))
    wide = dot(hit, one_hot(iota((held, rows), 0) == iota((held, rows), 1) // width))
    even = iota((8 * owners, rows), 0) % 2 == 0
    packed = dot(jnp.where(even, wide, 0.0).astype(BF16), latents[:, 0:128])
    packed = packed + dot(jnp.where(even, 0.0, wide).astype(BF16), latents[:, 128:256])
    owner = jnp.floor(slot_row * 0.5)
    hit = ((iota(shape, 0) // 8).astype(F32) == owner) & (sub == 4)
    packed = packed + dot(one_hot(hit), ranked)
    out_ref[...] = packed.astype(BF16).reshape(owners, 8, 128)


def unpack_messages(arrived, block_ref, field_ref):
    loaders = arrived.shape[0]
    slots = 2 * loaders
    flat = arrived.reshape(8 * loaders, 128)
    shape = (slots, 8 * loaders)
    base = 8 * (iota(shape, 0) // 2) + 2 * (iota(shape, 0) % 2)
    block_ref[:, 0:128] = dot(one_hot(iota(shape, 1) == base), flat).astype(BF16)
    block_ref[:, 128:256] = dot(one_hot(iota(shape, 1) == base + 1), flat).astype(BF16)
    both = dot(one_hot(iota(shape, 1) == 8 * (iota(shape, 0) // 2) + 4), flat)
    odd = iota((slots, META), 0) % 2 == 1
    fields = jnp.where(odd, pltpu.roll(both, META - 8, axis=1), both)
    pick = one_hot(iota((8, META), 0) == iota((8, META), 1))
    turned = dot_nt(pick, fields.astype(BF16))
    wide = jnp.concatenate([turned, jnp.zeros((8, META - slots), F32)], axis=1)
    field_ref[...] = wide.astype(BF16)


def sincos(angle):
    turns = jnp.floor(angle * (0.5 / math.pi) + 0.5)
    r = angle - turns * 6.28125
    r = r - turns * (2.0 * math.pi - 6.28125)
    z = r * r
    s = jnp.full_like(z, -1.0 / math.factorial(15))
    for n in (13, 11, 9, 7, 5, 3, 1):
        s = s * z + (1.0 if n % 4 == 1 else -1.0) / math.factorial(n)
    c = jnp.full_like(z, 1.0 / math.factorial(16))
    for n in (14, 12, 10, 8, 6, 4, 2, 0):
        c = c * z + (1.0 if n % 4 == 0 else -1.0) / math.factorial(n)
    return s * r, c


def axis_masks(shape):
    pair = iota(shape, 1) % 64
    return pair < 22, (pair >= 22) & (pair < 43), pair >= 43


def swap_halves(u):
    lane = iota(u.shape, 1)
    turned = pltpu.roll(u, 64, axis=1)
    return jnp.where(lane < 64, -turned, turned)


def rotary_tables(freq):
    shape = (FIELDS, META)
    sub = iota(shape, 0)
    in_f, in_r, in_c = axis_masks(shape)
    step = jnp.where((sub == 1) & in_f, 1.0, 0.0)
    step = jnp.where(((sub == 2) & in_r) | ((sub == 3) & in_c), 2.0, step)
    rest = jnp.broadcast_to(freq, shape)
    tables = []
    for _ in range(3):
        part = rest.astype(BF16).astype(F32)
        rest = rest - part
        tables.append((step * part).astype(BF16))
    return jnp.concatenate(tables + [step.astype(BF16)], axis=1)


def token_weights(ew_ref, freq, first):
    base = ew_ref[:, first : first + 128]
    shape = (8, 128)
    in_f, in_r, in_c = axis_masks(shape)
    blocks = []
    for tok in range(4):
        offset = jnp.where(in_r, float(tok // 2), 0.0) + jnp.where(in_c, float(tok % 2), 0.0)
        s, c = sincos(jnp.broadcast_to(freq, shape) * offset)
        turned = base * c[0:1, :] + swap_halves(base) * s[0:1, :]
        blocks.append(jnp.concatenate([turned, swap_halves(turned)], axis=1))
    return jnp.concatenate(blocks, axis=0)


def from_fields(fields, tables):
    wide = dot_tn(fields, tables)
    angle = wide[:, 0:128] + wide[:, 128:256] + wide[:, 256:384]
    s, c = sincos(angle)
    return s, c, wide[:, 384:512]


def project_keys(batch, block_ref, field_ref, tables, wk, wv, keys_ref, vals_ref):
    blocks, slots, _ = block_ref.shape
    tiles = blocks * slots
    wide = [dot_tn(field_ref[i, :, 0:slots], tables) for i in range(blocks)]
    wide = jnp.concatenate(wide, axis=0)
    s, c = sincos(wide[:, 0:128] + wide[:, 128:256] + wide[:, 256:384])
    pos = wide[:, 384:512]
    pick = one_hot((iota((FIELDS, META), 0) == 4) & (iota((FIELDS, META), 1) == 0))
    live = jnp.concatenate([dot_tn(field_ref[i, :, 0:slots], pick) for i in range(blocks)], axis=0)
    dead = jnp.where(iota((tiles, META), 1) == 0, (live - 1.0) * BIG, 0.0).astype(BF16)
    lat = block_ref[...].reshape(tiles, 256)
    in_f, in_r, in_c = axis_masks((1, 128))
    for tok in range(4):
        at = (batch * 4 + tok) * tiles
        here = iota((256, 1), 0) // 64 == tok
        u = dot(lat, jnp.where(here, wk, 0.0).astype(BF16))
        k = u[:, 0:128] * c + u[:, 128:256] * s
        shift = jnp.where(in_r, float(tok // 2), 0.0) + jnp.where(in_c, float(tok % 2), 0.0)
        keys_ref[at : at + tiles, 0:128] = dead
        keys_ref[at : at + tiles, 128:256] = k.astype(BF16)
        keys_ref[at : at + tiles, 256:384] = (k * (pos + shift)).astype(BF16)
        vals_ref[at : at + tiles, :] = dot(lat, jnp.where(here, wv, 0.0).astype(BF16)).astype(BF16)


def project_queries(lat, fields, tables, wq):
    slots = lat.shape[0]
    tokens = 4 * slots
    taken = (iota((tokens, slots), 0) // 4).astype(F32) == fields[0:1, :].astype(F32)
    chosen = one_hot(taken & (fields[4:5, :].astype(F32) > 0.5))
    which = iota((tokens, 256), 0) % 4 == iota((tokens, 256), 1) // 64
    my_lat = jnp.where(which, dot(chosen, lat), 0.0).astype(BF16)
    my_fields = dot_nt(fields, chosen).astype(BF16)
    s, c, pos = from_fields(my_fields, tables)
    pick = one_hot(iota((FIELDS, META), 0) == 4)
    live = dot_tn(my_fields, pick)
    u = dot(my_lat, wq.astype(BF16))
    q = u[:, 0:128] * c + u[:, 128:256] * s
    in_f, in_r, in_c = axis_masks((tokens, 128))
    tok = iota((tokens, 128), 0) % 4
    pos = pos + jnp.where(in_r & (tok >= 2), 1.0, 0.0) + jnp.where(in_c & (tok % 2 == 1), 1.0, 0.0)
    lane0 = one_hot(iota((tokens, META), 1) == 0)
    scale = 128.0 ** (-0.5) * math.log2(math.e)
    q_ext = jnp.concatenate([lane0, (q * scale).astype(BF16)], axis=1)
    return q, q_ext, pos, live


def finish_attention(q, q_ext, pos, live, top, cot_ref, out_ref, keys_ref, vals_ref, score_ref):
    tokens = q.shape[0]
    keys = keys_ref.shape[0]
    chunk = min(512, keys)
    starts = range(0, keys, chunk)
    top = jnp.max(top, axis=1, keepdims=True)
    sums = jnp.zeros((tokens, chunk), F32)
    mixed = jnp.zeros((tokens, 128), F32)
    for at in starts:
        weights = jnp.exp2(score_ref[:, at : at + chunk] - top)
        score_ref[:, at : at + chunk] = weights
        sums = sums + weights
        mixed = mixed + dot(weights.astype(BF16), vals_ref[at : at + chunk, :])
    inv = 1.0 / jnp.sum(sums, axis=1, keepdims=True)
    mixed = mixed * inv
    out_ref[...] = (mixed * live).astype(BF16)
    cot = cot_ref[...]
    mean = jnp.sum(cot.astype(F32) * mixed, axis=1, keepdims=True)
    back = jnp.zeros((tokens, 256), F32)
    for at in starts:
        dprob = dot_nt(cot, vals_ref[at : at + chunk, :])
        dscore = score_ref[:, at : at + chunk] * (dprob - mean)
        back = back + dot(dscore.astype(BF16), keys_ref[at : at + chunk, 128:384])
    g = pltpu.roll(back[:, 0:128], 64, axis=1)
    gp = pltpu.roll(back[:, 128:256], 64, axis=1)
    terms = q * (pos * g - gp) * (inv * 128.0 ** (-0.5) * live)
    line = jnp.sum(terms, axis=0, keepdims=True)
    other = pltpu.roll(line, 64, axis=1)
    return jnp.where(iota((1, 128), 1) < 64, line - other, other - line)


def greet():
    me_dp, me_seq = lax.axis_index("dp"), lax.axis_index("seq")
    n_dp, n_seq = lax.axis_size("dp"), lax.axis_size("seq")
    barrier = pltpu.get_barrier_semaphore()

    def to_dp(i, _):
        peer = lax.rem(me_dp + i, n_dp)
        pl.semaphore_signal(barrier, inc=1, device_id=(peer, me_seq), device_id_type=MESH)
        return 0

    def to_seq(i, _):
        peer = lax.rem(me_seq + i, n_seq)
        pl.semaphore_signal(barrier, inc=1, device_id=(me_dp, peer), device_id_type=MESH)
        return 0

    lax.fori_loop(1, n_dp, to_dp, 0)
    lax.fori_loop(1, n_seq, to_seq, 0)
    return barrier, n_dp + n_seq - 2


def spread(axis, src_of, dst_ref, send_sem, recv_sem):
    me_dp, me_seq = lax.axis_index("dp"), lax.axis_index("seq")
    n = lax.axis_size(axis)
    me = lax.axis_index(axis)

    def copy(peer, slot):
        where = (peer, me_seq) if axis == "dp" else (me_dp, peer)
        return pltpu.make_async_remote_copy(
            src_ref=src_of(peer),
            dst_ref=dst_ref.at[slot],
            send_sem=send_sem.at[peer],
            recv_sem=recv_sem.at[slot],
            device_id=where,
            device_id_type=MESH,
        )

    def each(act):
        def body(i, _):
            act(lax.rem(me + i, n))
            return 0

        lax.fori_loop(1, n, body, 0)

    def start():
        each(lambda peer: copy(peer, me).start())

    def wait_recv():
        each(lambda peer: copy(peer, peer).wait_recv())

    def wait_send():
        each(lambda peer: copy(peer, me).wait_send())

    return start, wait_recv, wait_send


def fold_load(embed_ref, qkv_ref, unit, window, columns, sems):
    shard = qkv_ref.shape[0]
    wide = window.shape[1]
    first = (lax.axis_index("seq") * shard) // 128 * 128
    rows = pl.ds(pl.multiple_of(8 * (unit // 3), 8), 8)
    cols = pl.ds(pl.multiple_of(128 * (unit % 3), 128), 128)
    left = pltpu.make_async_copy(embed_ref.at[rows, pl.ds(pl.multiple_of(first, 128), wide)], window, sems.at[0])
    right = pltpu.make_async_copy(qkv_ref.at[:, cols], columns, sems.at[1])
    left.start()
    right.start()
    return left, right


def fold_partial(window, columns):
    shard = columns.shape[0]
    wide = window.shape[1]
    part = window[...].astype(F32)
    if wide != shard:
        odd = lax.axis_index("seq") % 2 == 1
        part = jnp.where(odd, pltpu.roll(part, wide - 64, axis=1), part)
    return dot(part[:, 0:shard].astype(BF16), columns[...])


def turn_weights(source, chans, taps, target):
    for slot, tap in enumerate(taps):
        part = source[:, tap * chans : (tap + 1) * chans].astype(F32)
        target[slot] = part.T.astype(BF16)


def whole_kernel(
    tiles_hbm,
    dest_hbm,
    meta_hbm,
    space_hbm,
    time_hbm,
    bias_hbm,
    latent_hbm,
    embed_hbm,
    qkv_hbm,
    freq_hbm,
    cot_hbm,
    out_ref,
    grad_ref,
    tiles,
    dest,
    meta,
    space_raw,
    time_raw,
    bias,
    latent,
    freq_in,
    cot,
    window,
    columns,
    load_sem,
    tile_sem,
    fold_sem,
    space,
    time,
    messages,
    arrived,
    blocks,
    fields,
    parts,
    unit_buf,
    unit_all,
    ew,
    keys_ref,
    vals_ref,
    score_ref,
    line,
    mid,
    by_seq,
    by_dp,
    part_send,
    part_recv,
    unit_send,
    unit_recv,
    msg_send,
    msg_recv,
    ring_send,
    ring_recv,
    seq_send,
    seq_recv,
    dp_send,
    dp_recv,
):
    me_dp, me_seq = lax.axis_index("dp"), lax.axis_index("seq")
    n_dp, n_seq = lax.axis_size("dp"), lax.axis_size("seq")
    held, _, height, width, chans = tiles.shape
    per = parts.shape[1]

    loads = []
    pairs = [(dest_hbm, dest), (meta_hbm, meta), (space_hbm, space_raw), (time_hbm, time_raw), (bias_hbm, bias)]
    pairs += [(latent_hbm, latent), (freq_hbm, freq_in), (cot_hbm, cot)]
    for i, (source, target) in enumerate(pairs):
        loads.append(pltpu.make_async_copy(source, target, load_sem.at[i]))
        loads[-1].start()
    folds = []
    for j in range(per):
        unit = lax.rem(me_dp * per + j, UNITS)
        folds.append(fold_load(embed_hbm, qkv_hbm, unit, window.at[j], columns.at[j], fold_sem.at[j]))
    chunks = []
    for i in range(height // 2):
        rows = pl.ds(2 * i, 2)
        chunks.append(pltpu.make_async_copy(tiles_hbm.at[:, :, rows], tiles.at[:, :, rows], tile_sem.at[i]))
        chunks[-1].start()
    barrier, count = greet()

    for load in loads:
        load.wait()
    for left, right in folds:
        left.wait()
        right.wait()
    for j in range(per):
        parts[me_seq, j] = fold_partial(window.at[j], columns.at[j])
    turn_weights(space_raw, chans, range(9), space)
    turn_weights(time_raw, chans, (1, 2), time)
    slot_row, ranked = place_tiles(dest, meta, n_dp)
    latent_wide = jnp.concatenate([latent[...]] * 16, axis=0)

    start_parts, recv_parts, sent_parts = spread("seq", lambda peer: parts.at[me_seq], parts, part_send, part_recv)
    start_msgs, recv_msgs, sent_msgs = spread("dp", lambda peer: messages.at[peer], arrived, msg_send, msg_recv)
    start_units, recv_units, sent_units = spread("dp", lambda peer: unit_buf, unit_all, unit_send, unit_recv)
    start_seq, recv_seq, sent_seq = spread("seq", lambda peer: line, by_seq, seq_send, seq_recv)
    start_dp, recv_dp, sent_dp = spread("dp", lambda peer: mid, by_dp, dp_send, dp_recv)

    total = None
    for h in range(height // 2):
        if h == 0:
            chunks[0].wait()
        if h + 1 < height // 2:
            chunks[h + 1].wait()
        part = encode_rows(h, tiles, space, time, bias[...], latent_wide)
        total = part if total is None else total + part
        if h == height // 4:
            pl.semaphore_wait(barrier, count)
            start_parts()
    pack_messages(total, slot_row, ranked, width, messages)
    start_msgs()
    arrived[me_dp] = messages[me_dp]
    recv_msgs()
    unpack_messages(arrived[...], blocks.at[0], fields.at[0])

    far = {1: n_seq // 2, -1: (n_seq - 1) // 2}

    def slot_at(way, distance):
        return 2 * distance - 1 if way == 1 else 2 * distance

    def hop(way, source, distance, links):
        to = lax.rem(me_seq + way * links + n_seq, n_seq)
        slot = slot_at(way, distance)
        copies = []
        for kind, buf in enumerate((blocks, fields)):
            copies.append(
                pltpu.make_async_remote_copy(
                    src_ref=buf.at[source],
                    dst_ref=buf.at[slot],
                    send_sem=ring_send.at[kind, slot],
                    recv_sem=ring_recv.at[kind, slot],
                    device_id=(me_dp, to),
                    device_id_type=MESH,
                )
            )
        return copies

    sends = []

    def send(way, source, distance, links):
        for copy in hop(way, source, distance, links):
            copy.start()
            sends.append(copy)

    def receive(distance):
        for way in (1, -1):
            if distance <= far[way]:
                for copy in hop(way, 0, distance, 1):
                    copy.wait_recv()
                if distance + 2 <= far[way]:
                    send(way, slot_at(way, distance), distance + 2, 2)

    for distance in (1, 2):
        for way in (1, -1):
            if distance <= far[way]:
                send(way, 0, distance, distance)

    recv_parts()
    unit_buf[...] = jnp.sum(parts[...], axis=0)
    unit_all[me_dp] = unit_buf[...]
    start_units()

    group = min(4, n_seq)
    slots = blocks.shape[1]
    tokens = 4 * slots
    last = (n_seq // group - 1) * group
    got = 1
    while slot_at(-1, got) < last or slot_at(1, got) < last:
        receive(got)
        got += 1
    recv_units()
    for unit in range(UNITS):
        ew[8 * (unit // 3) : 8 * (unit // 3) + 8, 128 * (unit % 3) : 128 * (unit % 3) + 128] = unit_all[unit // per, unit % per]

    freq = jnp.concatenate([freq_in[...], freq_in[...]], axis=1)
    tables = rotary_tables(freq)
    wq = token_weights(ew, freq, 0)
    wk = token_weights(ew, freq, 128)
    wv = jnp.concatenate([ew[:, 256:384]] * 4, axis=0)
    q, q_ext, pos, live = project_queries(blocks[0], fields[0, :, 0:slots], tables, wq)
    step = group * tokens
    top = jnp.full((tokens, step), -jnp.inf, F32)
    for batch in range(n_seq // group):
        if batch == n_seq // group - 1:
            while got <= far[1]:
                receive(got)
                got += 1
        part = pl.ds(batch * group, group)
        project_keys(batch, blocks.at[part], fields.at[part], tables, wk, wv, keys_ref, vals_ref)
        scores = dot_nt(q_ext, keys_ref[batch * step : (batch + 1) * step, 0:256])
        score_ref[:, batch * step : (batch + 1) * step] = scores
        top = jnp.maximum(top, scores)
    line[...] = finish_attention(q, q_ext, pos, live, top, cot, out_ref, keys_ref, vals_ref, score_ref)

    start_seq()
    by_seq[me_seq] = line[...]
    recv_seq()
    mid[...] = jnp.sum(by_seq[...], axis=0)
    start_dp()
    by_dp[me_dp] = mid[...]
    for copy in sends:
        copy.wait_send()
    sent_msgs()
    sent_parts()
    sent_units()
    sent_seq()
    recv_dp()
    grad_ref[...] = jnp.sum(by_dp[...], axis=0)[:, 0 : grad_ref.shape[1]]
    sent_dp()


def per_device(
    tiles,
    tile_dest,
    tile_meta,
    space_weight,
    time_weight,
    conv_bias,
    latent_weight,
    embed_weight,
    qkv_weight,
    rope_freq,
    cotangent,
):
    n_dp, n_seq = lax.axis_size("dp"), lax.axis_size("seq")
    chans = tiles.shape[-1]
    slots = 2 * n_dp
    tokens = 4 * slots
    keys = tokens * n_seq
    per = -(-UNITS // n_dp)
    shard = qkv_weight.shape[0]
    pairs = rope_freq.shape[0]
    operands = (
        tiles,
        tile_dest[None, :],
        tile_meta.T,
        space_weight.T,
        time_weight.T,
        conv_bias[None, :],
        latent_weight.T,
        embed_weight,
        qkv_weight,
        rope_freq[None, :],
        cotangent,
    )
    dma = pltpu.SemaphoreType.DMA
    buf = pltpu.VMEM
    local = [operands[i] for i in (0, 1, 2, 3, 4, 5, 6, 9, 10)]
    scratch = [buf(a.shape, a.dtype) for a in local]
    scratch += [
        buf((per, 8, -(-shard // 128) * 128), BF16),
        buf((per, shard, 128), BF16),
        dma((8,)),
        dma((tiles.shape[2] // 2,)),
        dma((per, 2)),
        buf((9, chans, chans), BF16),
        buf((2, chans, chans), BF16),
        buf((n_dp, 8, 128), BF16),
        buf((n_dp, 8, 128), BF16),
        buf((n_seq, slots, 256), BF16),
        buf((n_seq, FIELDS, META), BF16),
        buf((n_seq, per, 8, 128), F32),
        buf((per, 8, 128), F32),
        buf((n_dp, per, 8, 128), F32),
        buf((64, 384), F32),
        buf((keys, 384), BF16),
        buf((keys, 128), BF16),
        buf((tokens, keys), F32),
        buf((1, 128), F32),
        buf((1, 128), F32),
        buf((n_seq, 1, 128), F32),
        buf((n_dp, 1, 128), F32),
        dma((n_seq,)),
        dma((n_seq,)),
        dma((n_dp,)),
        dma((n_dp,)),
        dma((n_dp,)),
        dma((n_dp,)),
        dma((2, n_seq)),
        dma((2, n_seq)),
        dma((n_seq,)),
        dma((n_seq,)),
        dma((n_dp,)),
        dma((n_dp,)),
    ]
    vmem = pl.BlockSpec(memory_space=pltpu.VMEM)
    attended, grad = pl.pallas_call(
        whole_kernel,
        out_shape=(
            jax.ShapeDtypeStruct((tokens, 128), BF16),
            jax.ShapeDtypeStruct((1, pairs), F32),
        ),
        in_specs=[pl.BlockSpec(memory_space=pltpu.HBM)] * len(operands),
        out_specs=(vmem, vmem),
        scratch_shapes=scratch,
        compiler_params=pltpu.CompilerParams(
            vmem_limit_bytes=56 << 20, collective_id=0, has_side_effects=True
        ),
    )(*operands)
    return attended, grad[0]


def solution(mesh):
    both = ("dp", "seq")
    specs = (
        P(both, None, None, None, None),
        P(both),
        P(both, None),
        P(),
        P(),
        P(),
        P(),
        P(),
        P("seq", None),
        P(),
        P(both, None),
    )
    return jax.shard_map(
        per_device,
        mesh=mesh,
        in_specs=specs,
        out_specs=(P(both, None), P()),
        check_vma=False,
    )
```

```python
import math

import jax
import jax.numpy as jnp
from jax import lax
from jax.experimental import pallas as pl
from jax.experimental.pallas import tpu as pltpu
from jax.sharding import PartitionSpec as P

F32 = jnp.float32
BF16 = jnp.bfloat16
MESH = pl.DeviceIdType.MESH
META = 128
BIG = 1e30
UNITS = 24
FIELDS = 8
STRIDE = 2


def iota(shape, dim):
    return lax.broadcasted_iota(jnp.int32, shape, dim)


def dot(a, b):
    return jnp.dot(a, b, preferred_element_type=F32)


def dot_nt(a, b):
    return lax.dot_general(a, b, (((1,), (1,)), ((), ())), preferred_element_type=F32)


def dot_tn(a, b):
    return lax.dot_general(a, b, (((0,), (0,)), ((), ())), preferred_element_type=F32)


def one_hot(cond):
    return jnp.where(cond, 1.0, 0.0).astype(BF16)


def place_tiles(dest_ref, meta_ref, owners):
    held = dest_ref.shape[1]
    square = (held, held)
    row = jnp.broadcast_to(dest_ref[...].astype(F32), square)
    first, second = iota(square, 0), iota(square, 1)
    col = jnp.sum(jnp.where(first == second, row, 0.0), axis=1, keepdims=True)
    same = jnp.where(col == row, 1.0, 0.0)
    rank_row = jnp.sum(jnp.where(first < second, same, 0.0), axis=0, keepdims=True)
    rank_col = jnp.sum(jnp.where(second < first, same, 0.0), axis=1, keepdims=True)
    slot_row = 2.0 * row[0:1, :] + rank_row
    shape = (8, held)
    fields = jnp.concatenate([meta_ref[...].astype(F32), jnp.ones((4, held), F32)], axis=0)
    fields = jnp.where(iota(shape, 0) < 5, fields, 0.0).astype(BF16)
    pick = one_hot(iota((8, META), 0) == iota((8, META), 1) % 8)
    lanes = dot_tn(fields, pick)
    ranked = jnp.where((iota((held, META), 1) // 8).astype(F32) == rank_col, lanes, 0.0).astype(BF16)
    return slot_row, ranked


def encode_rows(h, tiles_ref, space_ref, time_ref, bias, latent):
    held, frames, height, width, chans = tiles_ref.shape
    rows = held * width
    lat_wide = latent.shape[0]
    deep = space_ref.shape[1] // 3
    pad = jnp.zeros((held * frames * width, deep - chans), BF16)
    taps = []
    for src in range(2 * h, min(2 * h + 3, height)):
        taps += [tiles_ref[:, :, src].reshape(held * frames * width, chans), pad]
    x = jnp.concatenate(taps, axis=1)
    shifted = [dot(x, space_ref[col_off, 0 : x.shape[1], :]) for col_off in range(3)]
    y0, y1, y2 = [y.reshape(held * frames, width, chans) for y in shifted]
    y1 = pltpu.roll(y1, width - 1, axis=1)
    edge = iota((1, width, chans), 1) < width - 2
    y2 = jnp.where(edge, pltpu.roll(y2, width - 2, axis=1), 0.0)
    spatial = (y0 + y1 + y2).reshape(held, frames, width, chans)
    first = spatial[:, 0].reshape(rows, chans).astype(BF16)
    second = spatial[:, 1].reshape(rows, chans).astype(BF16)
    summed = dot(first, time_ref[0]) + dot(second, time_ref[1]) + bias
    feats = (summed / (1.0 + jnp.exp(-summed))).astype(BF16)
    lane = iota((rows, lat_wide), 1)
    lane_h = 2 * (lane // 128) + (lane // 32) % 2
    lane_w = 2 * ((lane // 64) % 2) + (lane // 16) % 2
    keep = (lane_h == h) & (2 * lane_w == iota((rows, lat_wide), 0) % width)
    return jnp.where(keep, dot_nt(feats, latent), 0.0)


def packing(slot_row, rows, width, owners):
    held = slot_row.shape[1]
    shape = (8 * owners, held)
    sub = iota(shape, 0) % 8
    mine = (2 * (iota(shape, 0) // 8) + sub // 2).astype(F32) == slot_row
    hit = one_hot(mine & (sub < 4))
    wide = dot(hit, one_hot(iota((held, rows), 0) == iota((held, rows), 1) // width))
    even = iota((8 * owners, rows), 0) % 2 == 0
    owner = jnp.floor(slot_row * 0.5)
    named = one_hot(((iota(shape, 0) // 8).astype(F32) == owner) & (sub == 4))
    return jnp.where(even, wide, 0.0).astype(BF16), jnp.where(even, 0.0, wide).astype(BF16), named


def pack_messages(latents, picks, ranked, out_ref):
    owners = out_ref.shape[0]
    latents = latents.astype(BF16)
    packed = dot(picks[0], latents[:, 0:128]) + dot(picks[1], latents[:, 128:256]) + dot(picks[2], ranked)
    out_ref[...] = packed.astype(BF16).reshape(owners, 8, 128)


def unpack_messages(arrived, block_ref, field_ref):
    loaders = arrived.shape[0]
    slots = 2 * loaders
    flat = arrived.reshape(8 * loaders, 128)
    shape = (slots, 8 * loaders)
    base = 8 * (iota(shape, 0) // 2) + 2 * (iota(shape, 0) % 2)
    block_ref[:, 0:128] = dot(one_hot(iota(shape, 1) == base), flat).astype(BF16)
    block_ref[:, 128:256] = dot(one_hot(iota(shape, 1) == base + 1), flat).astype(BF16)
    both = dot(one_hot(iota(shape, 1) == 8 * (iota(shape, 0) // 2) + 4), flat)
    odd = iota((slots, META), 0) % 2 == 1
    fields = jnp.where(odd, pltpu.roll(both, META - 8, axis=1), both)
    pick = one_hot(iota((8, META), 0) == iota((8, META), 1))
    turned = dot_nt(pick, fields.astype(BF16))
    wide = jnp.concatenate([turned, jnp.zeros((8, META - slots), F32)], axis=1)
    field_ref[...] = wide.astype(BF16)


def sincos(angle):
    turns = jnp.floor(angle * (0.5 / math.pi) + 0.5)
    r = angle - turns * 6.28125
    r = r - turns * (2.0 * math.pi - 6.28125)
    z = r * r
    s = jnp.full_like(z, -1.0 / math.factorial(15))
    for n in (13, 11, 9, 7, 5, 3, 1):
        s = s * z + (1.0 if n % 4 == 1 else -1.0) / math.factorial(n)
    c = jnp.full_like(z, 1.0 / math.factorial(16))
    for n in (14, 12, 10, 8, 6, 4, 2, 0):
        c = c * z + (1.0 if n % 4 == 0 else -1.0) / math.factorial(n)
    return s * r, c


def axis_masks(shape):
    pair = iota(shape, 1) % 64
    return pair < 22, (pair >= 22) & (pair < 43), pair >= 43


def swap_halves(u):
    lane = iota(u.shape, 1)
    turned = pltpu.roll(u, 64, axis=1)
    return jnp.where(lane < 64, -turned, turned)


def rotary_tables(freq):
    shape = (FIELDS, META)
    sub = iota(shape, 0)
    in_f, in_r, in_c = axis_masks(shape)
    step = jnp.where((sub == 1) & in_f, 1.0, 0.0)
    step = jnp.where(((sub == 2) & in_r) | ((sub == 3) & in_c), 2.0, step)
    rest = jnp.broadcast_to(freq, shape)
    tables = []
    for _ in range(3):
        part = rest.astype(BF16).astype(F32)
        rest = rest - part
        tables.append((step * part).astype(BF16))
    return jnp.concatenate(tables + [step.astype(BF16)], axis=1)


def token_weights(ew_ref, freq, first):
    base = ew_ref[:, first : first + 128]
    shape = (8, 128)
    in_f, in_r, in_c = axis_masks(shape)
    blocks = []
    for tok in range(4):
        offset = jnp.where(in_r, float(tok // 2), 0.0) + jnp.where(in_c, float(tok % 2), 0.0)
        s, c = sincos(jnp.broadcast_to(freq, shape) * offset)
        turned = base * c[0:1, :] + swap_halves(base) * s[0:1, :]
        blocks.append(jnp.concatenate([turned, swap_halves(turned)], axis=1))
    return jnp.concatenate(blocks, axis=0)


def from_fields(fields, tables):
    wide = dot_tn(fields, tables)
    angle = wide[:, 0:128] + wide[:, 128:256] + wide[:, 256:384]
    s, c = sincos(angle)
    return s, c, wide[:, 384:512]


def project_keys(batch, block_ref, field_ref, tables, wk, wv, keys_ref, vals_ref):
    blocks, slots, _ = block_ref.shape
    tiles = blocks * slots
    wide = [dot_tn(field_ref[i, :, 0:slots], tables) for i in range(blocks)]
    wide = jnp.concatenate(wide, axis=0)
    s, c = sincos(wide[:, 0:128] + wide[:, 128:256] + wide[:, 256:384])
    pos = wide[:, 384:512]
    pick = one_hot((iota((FIELDS, META), 0) == 4) & (iota((FIELDS, META), 1) == 0))
    live = jnp.concatenate([dot_tn(field_ref[i, :, 0:slots], pick) for i in range(blocks)], axis=0)
    dead = jnp.where(iota((tiles, META), 1) == 0, (live - 1.0) * BIG, 0.0).astype(BF16)
    lat = block_ref[...].reshape(tiles, 256)
    in_f, in_r, in_c = axis_masks((1, 128))
    for tok in range(4):
        at = (batch * 4 + tok) * tiles
        here = iota((256, 1), 0) // 64 == tok
        u = dot(lat, jnp.where(here, wk, 0.0).astype(BF16))
        k = u[:, 0:128] * c + u[:, 128:256] * s
        shift = jnp.where(in_r, float(tok // 2), 0.0) + jnp.where(in_c, float(tok % 2), 0.0)
        keys_ref[at : at + tiles, 0:128] = dead
        keys_ref[at : at + tiles, 128:256] = k.astype(BF16)
        keys_ref[at : at + tiles, 256:384] = (k * (pos + shift)).astype(BF16)
        vals_ref[at : at + tiles, :] = dot(lat, jnp.where(here, wv, 0.0).astype(BF16)).astype(BF16)


def project_queries(lat, fields, tables, wq):
    slots = lat.shape[0]
    tokens = 4 * slots
    taken = (iota((tokens, slots), 0) // 4).astype(F32) == fields[0:1, :].astype(F32)
    chosen = one_hot(taken & (fields[4:5, :].astype(F32) > 0.5))
    which = iota((tokens, 256), 0) % 4 == iota((tokens, 256), 1) // 64
    my_lat = jnp.where(which, dot(chosen, lat), 0.0).astype(BF16)
    my_fields = dot_nt(fields, chosen).astype(BF16)
    s, c, pos = from_fields(my_fields, tables)
    pick = one_hot(iota((FIELDS, META), 0) == 4)
    live = dot_tn(my_fields, pick)
    u = dot(my_lat, wq.astype(BF16))
    q = u[:, 0:128] * c + u[:, 128:256] * s
    in_f, in_r, in_c = axis_masks((tokens, 128))
    tok = iota((tokens, 128), 0) % 4
    pos = pos + jnp.where(in_r & (tok >= 2), 1.0, 0.0) + jnp.where(in_c & (tok % 2 == 1), 1.0, 0.0)
    lane0 = one_hot(iota((tokens, META), 1) == 0)
    scale = 128.0 ** (-0.5) * math.log2(math.e)
    q_ext = jnp.concatenate([lane0, (q * scale).astype(BF16)], axis=1)
    return q, q_ext, pos, live


def finish_attention(q, q_ext, pos, live, top, cot_ref, out_ref, keys_ref, vals_ref, score_ref):
    tokens = q.shape[0]
    keys = keys_ref.shape[0]
    chunk = min(512, keys)
    starts = range(0, keys, chunk)
    top = jnp.max(top, axis=1, keepdims=True)
    sums = jnp.zeros((tokens, chunk), F32)
    mixed = jnp.zeros((tokens, 128), F32)
    for at in starts:
        weights = jnp.exp2(score_ref[:, at : at + chunk] - top)
        score_ref[:, at : at + chunk] = weights
        sums = sums + weights
        mixed = mixed + dot(weights.astype(BF16), vals_ref[at : at + chunk, :])
    inv = 1.0 / jnp.sum(sums, axis=1, keepdims=True)
    mixed = mixed * inv
    out_ref[...] = mixed * live
    cot = cot_ref[...]
    mean = jnp.sum(cot.astype(F32) * mixed, axis=1, keepdims=True)
    back = jnp.zeros((tokens, 256), F32)
    for at in starts:
        dprob = dot_nt(cot, vals_ref[at : at + chunk, :])
        dscore = score_ref[:, at : at + chunk] * (dprob - mean)
        back = back + dot(dscore.astype(BF16), keys_ref[at : at + chunk, 128:384])
    g = pltpu.roll(back[:, 0:128], 64, axis=1)
    gp = pltpu.roll(back[:, 128:256], 64, axis=1)
    terms = q * (pos * g - gp) * (inv * 128.0 ** (-0.5) * live)
    line = jnp.sum(terms, axis=0, keepdims=True)
    other = pltpu.roll(line, 64, axis=1)
    return jnp.where(iota((1, 128), 1) < 64, line - other, other - line)


def greet():
    me_dp, me_seq = lax.axis_index("dp"), lax.axis_index("seq")
    n_dp, n_seq = lax.axis_size("dp"), lax.axis_size("seq")
    barrier = pltpu.get_barrier_semaphore()

    def to_dp(i, _):
        peer = lax.rem(me_dp + i, n_dp)
        pl.semaphore_signal(barrier, inc=1, device_id=(peer, me_seq), device_id_type=MESH)
        return 0

    def to_seq(i, _):
        peer = lax.rem(me_seq + i, n_seq)
        pl.semaphore_signal(barrier, inc=1, device_id=(me_dp, peer), device_id_type=MESH)
        return 0

    lax.fori_loop(1, n_dp, to_dp, 0)
    lax.fori_loop(1, n_seq, to_seq, 0)
    return barrier, n_dp + n_seq - 2


def spread(axis, src_of, dst_ref, send_sem, recv_sem):
    me_dp, me_seq = lax.axis_index("dp"), lax.axis_index("seq")
    n = lax.axis_size(axis)
    me = lax.axis_index(axis)

    def copy(peer, source, target):
        return pltpu.make_async_remote_copy(
            src_ref=source,
            dst_ref=target,
            send_sem=send_sem,
            recv_sem=recv_sem,
            device_id=(peer, me_seq) if axis == "dp" else (me_dp, peer),
            device_id_type=MESH,
        )

    def start():
        for i in range(1, n):
            peer = lax.rem(me + i, n)
            copy(peer, src_of(peer), dst_ref.at[me]).start()

    others = dst_ref.at[pl.ds(0, n - 1)]

    def wait_recv():
        copy(lax.rem(me + 1, n), others, others).wait_recv()

    def wait_send():
        copy(lax.rem(me + 1, n), others, others).wait_send()

    return start, wait_recv, wait_send


def fold_load(embed_ref, qkv_ref, unit, window, columns, sems):
    shard = qkv_ref.shape[0]
    wide = window.shape[1]
    first = (lax.axis_index("seq") * shard) // 128 * 128
    rows = pl.ds(pl.multiple_of(8 * (unit // 3), 8), 8)
    cols = pl.ds(pl.multiple_of(128 * (unit % 3), 128), 128)
    left = pltpu.make_async_copy(embed_ref.at[rows, pl.ds(pl.multiple_of(first, 128), wide)], window, sems.at[0])
    right = pltpu.make_async_copy(qkv_ref.at[:, cols], columns, sems.at[1])
    left.start()
    right.start()
    return left, right


def fold_partial(window, columns):
    shard = columns.shape[0]
    wide = window.shape[1]
    part = window[...].astype(F32)
    if wide != shard:
        odd = lax.axis_index("seq") % 2 == 1
        part = jnp.where(odd, pltpu.roll(part, wide - 64, axis=1), part)
    return dot(part[:, 0:shard].astype(BF16), columns[...])


def turn_weights(source, chans, tap, target):
    part = source[:, tap * chans : (tap + 1) * chans].astype(F32)
    target[0:chans, :] = part.T.astype(BF16)
    rest = target.shape[0] - chans
    if rest:
        target[chans:, :] = jnp.zeros((rest, chans), BF16)


def whole_kernel(
    tiles_hbm,
    dest_hbm,
    meta_hbm,
    space_hbm,
    time_hbm,
    bias_hbm,
    latent_hbm,
    embed_hbm,
    qkv_hbm,
    freq_hbm,
    cot_hbm,
    out_ref,
    grad_ref,
    tiles,
    dest,
    meta,
    space_raw,
    time_raw,
    bias,
    latent,
    freq_in,
    cot,
    window,
    columns,
    load_sem,
    tile_sem,
    fold_sem,
    space,
    time,
    messages,
    arrived,
    blocks,
    fields,
    parts,
    unit_buf,
    unit_all,
    ew,
    keys_ref,
    vals_ref,
    score_ref,
    line,
    mid,
    by_seq,
    by_dp,
    part_send,
    part_recv,
    unit_send,
    unit_recv,
    msg_send,
    msg_recv,
    ring_send,
    ring_recv,
    seq_send,
    seq_recv,
    dp_send,
    dp_recv,
):
    me_dp, me_seq = lax.axis_index("dp"), lax.axis_index("seq")
    n_dp, n_seq = lax.axis_size("dp"), lax.axis_size("seq")
    held, _, height, width, chans = tiles.shape
    per = parts.shape[1]

    loads = []
    pairs = [(dest_hbm, dest), (meta_hbm, meta), (space_hbm, space_raw), (time_hbm, time_raw), (bias_hbm, bias)]
    pairs += [(latent_hbm, latent), (freq_hbm, freq_in), (cot_hbm, cot)]
    for i, (source, target) in enumerate(pairs):
        loads.append(pltpu.make_async_copy(source, target, load_sem.at[i]))
        loads[-1].start()
    folds = []
    for j in range(per):
        unit = lax.rem(me_dp * per + j, UNITS)
        folds.append(fold_load(embed_hbm, qkv_hbm, unit, window.at[j], columns.at[j], fold_sem.at[j]))
    chunks = []
    for i in range(height // 2):
        rows = pl.ds(2 * i, 2)
        chunks.append(pltpu.make_async_copy(tiles_hbm.at[:, :, rows], tiles.at[:, :, rows], tile_sem.at[i]))
        chunks[-1].start()
    barrier, count = greet()

    for load in loads:
        load.wait()
    slot_row, ranked = place_tiles(dest, meta, n_dp)
    picks = packing(slot_row, held * width, width, n_dp)
    deep = space.shape[1] // 3
    for tap in range(9):
        turn_weights(space_raw, chans, tap, space.at[tap % 3, pl.ds(deep * (tap // 3), deep)])
    for tap in (1, 2):
        turn_weights(time_raw, chans, tap, time.at[tap - 1])
    latent_wide = jnp.concatenate([latent[...]] * 16, axis=0)

    start_parts, recv_parts, sent_parts = spread("seq", lambda peer: parts.at[me_seq], parts, part_send, part_recv)
    start_msgs, recv_msgs, sent_msgs = spread("dp", lambda peer: messages.at[peer], arrived, msg_send, msg_recv)
    start_units, recv_units, sent_units = spread("dp", lambda peer: unit_buf, unit_all, unit_send, unit_recv)
    start_seq, recv_seq, sent_seq = spread("seq", lambda peer: line, by_seq, seq_send, seq_recv)
    start_dp, recv_dp, sent_dp = spread("dp", lambda peer: mid, by_dp, dp_send, dp_recv)

    total = None
    for h in range(height // 2):
        if h == 0:
            chunks[0].wait()
        if h + 1 < height // 2:
            chunks[h + 1].wait()
        part = encode_rows(h, tiles, space, time, bias[...], latent_wide)
        total = part if total is None else total + part
    pack_messages(total, picks, ranked, messages)
    pl.semaphore_wait(barrier, count)
    start_msgs()
    for left, right in folds:
        left.wait()
        right.wait()
    for j in range(per):
        parts[me_seq, j] = fold_partial(window.at[j], columns.at[j])
    start_parts()
    arrived[me_dp] = messages[me_dp]
    recv_msgs()
    unpack_messages(arrived[...], blocks.at[0], fields.at[0])

    far = {1: n_seq // 2, -1: (n_seq - 1) // 2}

    def slot_at(way, distance):
        return 2 * distance - 1 if way == 1 else 2 * distance

    def hop(way, source, distance, links):
        to = lax.rem(me_seq + way * links + n_seq, n_seq)
        slot = slot_at(way, distance)
        copies = []
        for kind, buf in enumerate((blocks, fields)):
            copies.append(
                pltpu.make_async_remote_copy(
                    src_ref=buf.at[source],
                    dst_ref=buf.at[slot],
                    send_sem=ring_send.at[kind, slot],
                    recv_sem=ring_recv.at[kind, slot],
                    device_id=(me_dp, to),
                    device_id_type=MESH,
                )
            )
        return copies

    sends = []

    def send(way, source, distance, links):
        for copy in hop(way, source, distance, links):
            copy.start()
            sends.append(copy)

    def receive(distance):
        for way in (1, -1):
            if distance <= far[way]:
                for copy in hop(way, 0, distance, 1):
                    copy.wait_recv()
                if distance + STRIDE <= far[way]:
                    send(way, slot_at(way, distance), distance + STRIDE, STRIDE)

    for distance in range(1, STRIDE + 1):
        for way in (1, -1):
            if distance <= far[way]:
                send(way, 0, distance, distance)

    recv_parts()
    unit_buf[...] = jnp.sum(parts[...], axis=0)
    unit_all[me_dp] = unit_buf[...]
    start_units()

    group = min(4, n_seq)
    slots = blocks.shape[1]
    tokens = 4 * slots
    last = (n_seq // group - 1) * group
    got = 1
    while slot_at(-1, got) < last or slot_at(1, got) < last:
        receive(got)
        got += 1
    recv_units()
    for unit in range(UNITS):
        ew[8 * (unit // 3) : 8 * (unit // 3) + 8, 128 * (unit % 3) : 128 * (unit % 3) + 128] = unit_all[unit // per, unit % per]

    freq = jnp.concatenate([freq_in[...], freq_in[...]], axis=1)
    tables = rotary_tables(freq)
    wq = token_weights(ew, freq, 0)
    wk = token_weights(ew, freq, 128)
    wv = jnp.concatenate([ew[:, 256:384]] * 4, axis=0)
    q, q_ext, pos, live = project_queries(blocks[0], fields[0, :, 0:slots], tables, wq)
    step = group * tokens
    top = jnp.full((tokens, step), -jnp.inf, F32)
    for batch in range(n_seq // group):
        if batch == n_seq // group - 1:
            while got <= far[1]:
                receive(got)
                got += 1
        part = pl.ds(batch * group, group)
        project_keys(batch, blocks.at[part], fields.at[part], tables, wk, wv, keys_ref, vals_ref)
        scores = dot_nt(q_ext, keys_ref[batch * step : (batch + 1) * step, 0:256])
        score_ref[:, batch * step : (batch + 1) * step] = scores
        top = jnp.maximum(top, scores)
    line[...] = finish_attention(q, q_ext, pos, live, top, cot, out_ref, keys_ref, vals_ref, score_ref)

    start_seq()
    by_seq[me_seq] = line[...]
    recv_seq()
    mid[...] = jnp.sum(by_seq[...], axis=0)
    start_dp()
    by_dp[me_dp] = mid[...]
    for copy in sends:
        copy.wait_send()
    sent_msgs()
    sent_parts()
    sent_units()
    sent_seq()
    recv_dp()
    grad_ref[...] = jnp.sum(by_dp[...], axis=0)[:, 0 : grad_ref.shape[1]]
    sent_dp()


def per_device(
    tiles,
    tile_dest,
    tile_meta,
    space_weight,
    time_weight,
    conv_bias,
    latent_weight,
    embed_weight,
    qkv_weight,
    rope_freq,
    cotangent,
):
    n_dp, n_seq = lax.axis_size("dp"), lax.axis_size("seq")
    chans = tiles.shape[-1]
    slots = 2 * n_dp
    tokens = 4 * slots
    keys = tokens * n_seq
    per = -(-UNITS // n_dp)
    shard = qkv_weight.shape[0]
    pairs = rope_freq.shape[0]
    operands = (
        tiles,
        tile_dest[None, :],
        tile_meta.T,
        space_weight.T,
        time_weight.T,
        conv_bias[None, :],
        latent_weight.T,
        embed_weight,
        qkv_weight,
        rope_freq[None, :],
        cotangent,
    )
    dma = pltpu.SemaphoreType.DMA
    buf = pltpu.VMEM
    local = [operands[i] for i in (0, 1, 2, 3, 4, 5, 6, 9, 10)]
    scratch = [buf(a.shape, a.dtype) for a in local]
    scratch += [
        buf((per, 8, -(-shard // 128) * 128), BF16),
        buf((per, shard, 128), BF16),
        dma((8,)),
        dma((tiles.shape[2] // 2,)),
        dma((per, 2)),
        buf((3, 3 * 256, chans), BF16),
        buf((2, chans, chans), BF16),
        buf((n_dp, 8, 128), BF16),
        buf((n_dp, 8, 128), BF16),
        buf((n_seq, slots, 256), BF16),
        buf((n_seq, FIELDS, META), BF16),
        buf((n_seq, per, 8, 128), F32),
        buf((per, 8, 128), F32),
        buf((n_dp, per, 8, 128), F32),
        buf((64, 384), F32),
        buf((keys, 384), BF16),
        buf((keys, 128), BF16),
        buf((tokens, keys), F32),
        buf((1, 128), F32),
        buf((1, 128), F32),
        buf((n_seq, 1, 128), F32),
        buf((n_dp, 1, 128), F32),
        dma(()),
        dma(()),
        dma(()),
        dma(()),
        dma(()),
        dma(()),
        dma((2, n_seq)),
        dma((2, n_seq)),
        dma(()),
        dma(()),
        dma(()),
        dma(()),
    ]
    vmem = pl.BlockSpec(memory_space=pltpu.VMEM)
    attended, grad = pl.pallas_call(
        whole_kernel,
        out_shape=(
            jax.ShapeDtypeStruct((tokens, 128), F32),
            jax.ShapeDtypeStruct((1, pairs), F32),
        ),
        in_specs=[pl.BlockSpec(memory_space=pltpu.HBM)] * len(operands),
        out_specs=(vmem, vmem),
        scratch_shapes=scratch,
        compiler_params=pltpu.CompilerParams(
            vmem_limit_bytes=24 << 20, collective_id=0, has_side_effects=True
        ),
    )(*[pltpu.with_memory_space_constraint(a, pltpu.HBM) for a in operands])
    return attended.astype(BF16), grad[0]


def solution(mesh):
    both = ("dp", "seq")
    specs = (
        P(both, None, None, None, None),
        P(both),
        P(both, None),
        P(),
        P(),
        P(),
        P(),
        P(),
        P("seq", None),
        P(),
        P(both, None),
    )
    return jax.shard_map(
        per_device,
        mesh=mesh,
        in_specs=specs,
        out_specs=(P(both, None), P()),
        check_vma=False,
    )
```

```python
import math

import jax
import jax.numpy as jnp
from jax import lax
from jax.experimental import pallas as pl
from jax.experimental.pallas import tpu as pltpu
from jax.sharding import PartitionSpec as P

F32 = jnp.float32
BF16 = jnp.bfloat16
MESH = pl.DeviceIdType.MESH
META = 128
BIG = 1e30
UNITS = 24
FIELDS = 8
STRIDE = 2


def iota(shape, dim):
    return lax.broadcasted_iota(jnp.int32, shape, dim)


def dot(a, b):
    return jnp.dot(a, b, preferred_element_type=F32)


def dot_nt(a, b):
    return lax.dot_general(a, b, (((1,), (1,)), ((), ())), preferred_element_type=F32)


def dot_tn(a, b):
    return lax.dot_general(a, b, (((0,), (0,)), ((), ())), preferred_element_type=F32)


def one_hot(cond):
    return jnp.where(cond, 1.0, 0.0).astype(BF16)


def place_tiles(dest_ref, meta_ref, owners):
    held = dest_ref.shape[1]
    square = (held, held)
    row = jnp.broadcast_to(dest_ref[...].astype(F32), square)
    first, second = iota(square, 0), iota(square, 1)
    col = jnp.sum(jnp.where(first == second, row, 0.0), axis=1, keepdims=True)
    same = jnp.where(col == row, 1.0, 0.0)
    rank_row = jnp.sum(jnp.where(first < second, same, 0.0), axis=0, keepdims=True)
    rank_col = jnp.sum(jnp.where(second < first, same, 0.0), axis=1, keepdims=True)
    slot_row = 2.0 * row[0:1, :] + rank_row
    shape = (8, held)
    fields = jnp.concatenate([meta_ref[...].astype(F32), jnp.ones((4, held), F32)], axis=0)
    fields = jnp.where(iota(shape, 0) < 5, fields, 0.0).astype(BF16)
    pick = one_hot(iota((8, META), 0) == iota((8, META), 1) % 8)
    lanes = dot_tn(fields, pick)
    ranked = jnp.where((iota((held, META), 1) // 8).astype(F32) == rank_col, lanes, 0.0).astype(BF16)
    return slot_row, ranked


def encode_rows(h, tiles_ref, space_ref, time_ref, bias, latent):
    held, frames, height, width, chans = tiles_ref.shape
    rows = held * width
    lat_wide = latent.shape[0]
    deep = space_ref.shape[1] // 3
    pad = jnp.zeros((held * frames * width, deep - chans), BF16)
    taps = []
    for src in range(2 * h, min(2 * h + 3, height)):
        taps += [tiles_ref[:, :, src].reshape(held * frames * width, chans), pad]
    x = jnp.concatenate(taps, axis=1)
    shifted = [dot(x, space_ref[col_off, 0 : x.shape[1], :]) for col_off in range(3)]
    y0, y1, y2 = [y.reshape(held * frames, width, chans) for y in shifted]
    y1 = pltpu.roll(y1, width - 1, axis=1)
    edge = iota((1, width, chans), 1) < width - 2
    y2 = jnp.where(edge, pltpu.roll(y2, width - 2, axis=1), 0.0)
    spatial = (y0 + y1 + y2).reshape(held, frames, width, chans)
    first = spatial[:, 0].reshape(rows, chans).astype(BF16)
    second = spatial[:, 1].reshape(rows, chans).astype(BF16)
    summed = dot(first, time_ref[0]) + dot(second, time_ref[1]) + bias
    feats = (summed / (1.0 + jnp.exp(-summed))).astype(BF16)
    lane = iota((rows, lat_wide), 1)
    lane_h = 2 * (lane // 128) + (lane // 32) % 2
    lane_w = 2 * ((lane // 64) % 2) + (lane // 16) % 2
    keep = (lane_h == h) & (2 * lane_w == iota((rows, lat_wide), 0) % width)
    return jnp.where(keep, dot_nt(feats, latent), 0.0)


def packing(slot_row, rows, width, owners):
    held = slot_row.shape[1]
    shape = (8 * owners, held)
    sub = iota(shape, 0) % 8
    mine = (2 * (iota(shape, 0) // 8) + sub // 2).astype(F32) == slot_row
    hit = one_hot(mine & (sub < 4))
    wide = dot(hit, one_hot(iota((held, rows), 0) == iota((held, rows), 1) // width))
    even = iota((8 * owners, rows), 0) % 2 == 0
    owner = jnp.floor(slot_row * 0.5)
    named = one_hot(((iota(shape, 0) // 8).astype(F32) == owner) & (sub == 4))
    return jnp.where(even, wide, 0.0).astype(BF16), jnp.where(even, 0.0, wide).astype(BF16), named


def pack_messages(latents, picks, ranked, out_ref):
    owners = out_ref.shape[0]
    latents = latents.astype(BF16)
    packed = dot(picks[0], latents[:, 0:128]) + dot(picks[1], latents[:, 128:256]) + dot(picks[2], ranked)
    out_ref[...] = packed.astype(BF16).reshape(owners, 8, 128)


def unpack_messages(arrived, block_ref, field_ref):
    loaders = arrived.shape[0]
    slots = 2 * loaders
    flat = arrived.reshape(8 * loaders, 128)
    shape = (slots, 8 * loaders)
    base = 8 * (iota(shape, 0) // 2) + 2 * (iota(shape, 0) % 2)
    block_ref[:, 0:128] = dot(one_hot(iota(shape, 1) == base), flat).astype(BF16)
    block_ref[:, 128:256] = dot(one_hot(iota(shape, 1) == base + 1), flat).astype(BF16)
    both = dot(one_hot(iota(shape, 1) == 8 * (iota(shape, 0) // 2) + 4), flat)
    odd = iota((slots, META), 0) % 2 == 1
    fields = jnp.where(odd, pltpu.roll(both, META - 8, axis=1), both)
    pick = one_hot(iota((8, META), 0) == iota((8, META), 1))
    turned = dot_nt(pick, fields.astype(BF16))
    wide = jnp.concatenate([turned, jnp.zeros((8, META - slots), F32)], axis=1)
    field_ref[...] = wide.astype(BF16)


def sincos(angle):
    turns = jnp.floor(angle * (0.5 / math.pi) + 0.5)
    r = angle - turns * 6.28125
    r = r - turns * (2.0 * math.pi - 6.28125)
    z = r * r
    s = jnp.full_like(z, -1.0 / math.factorial(15))
    for n in (13, 11, 9, 7, 5, 3, 1):
        s = s * z + (1.0 if n % 4 == 1 else -1.0) / math.factorial(n)
    c = jnp.full_like(z, 1.0 / math.factorial(16))
    for n in (14, 12, 10, 8, 6, 4, 2, 0):
        c = c * z + (1.0 if n % 4 == 0 else -1.0) / math.factorial(n)
    return s * r, c


def axis_masks(shape):
    pair = iota(shape, 1) % 64
    return pair < 22, (pair >= 22) & (pair < 43), pair >= 43


def swap_halves(u):
    lane = iota(u.shape, 1)
    turned = pltpu.roll(u, 64, axis=1)
    return jnp.where(lane < 64, -turned, turned)


def rotary_tables(freq):
    shape = (FIELDS, META)
    sub = iota(shape, 0)
    in_f, in_r, in_c = axis_masks(shape)
    step = jnp.where((sub == 1) & in_f, 1.0, 0.0)
    step = jnp.where(((sub == 2) & in_r) | ((sub == 3) & in_c), 2.0, step)
    rest = jnp.broadcast_to(freq, shape)
    tables = []
    for _ in range(3):
        part = rest.astype(BF16).astype(F32)
        rest = rest - part
        tables.append((step * part).astype(BF16))
    return jnp.concatenate(tables + [step.astype(BF16)], axis=1)


def token_weights(ew_ref, freq, first):
    base = ew_ref[:, first : first + 128]
    shape = (8, 128)
    in_f, in_r, in_c = axis_masks(shape)
    blocks = []
    for tok in range(4):
        offset = jnp.where(in_r, float(tok // 2), 0.0) + jnp.where(in_c, float(tok % 2), 0.0)
        s, c = sincos(jnp.broadcast_to(freq, shape) * offset)
        turned = base * c[0:1, :] + swap_halves(base) * s[0:1, :]
        blocks.append(jnp.concatenate([turned, swap_halves(turned)], axis=1))
    return jnp.concatenate(blocks, axis=0)


def from_fields(fields, tables):
    wide = dot_tn(fields, tables)
    angle = wide[:, 0:128] + wide[:, 128:256] + wide[:, 256:384]
    s, c = sincos(angle)
    return s, c, wide[:, 384:512]


def project_keys(batch, block_ref, field_ref, tables, wk, wv, keys_ref, vals_ref):
    blocks, slots, _ = block_ref.shape
    tiles = blocks * slots
    wide = [dot_tn(field_ref[i, :, 0:slots], tables) for i in range(blocks)]
    wide = jnp.concatenate(wide, axis=0)
    s, c = sincos(wide[:, 0:128] + wide[:, 128:256] + wide[:, 256:384])
    pos = wide[:, 384:512]
    pick = one_hot((iota((FIELDS, META), 0) == 4) & (iota((FIELDS, META), 1) == 0))
    live = jnp.concatenate([dot_tn(field_ref[i, :, 0:slots], pick) for i in range(blocks)], axis=0)
    dead = jnp.where(iota((tiles, META), 1) == 0, (live - 1.0) * BIG, 0.0).astype(BF16)
    lat = block_ref[...].reshape(tiles, 256)
    in_f, in_r, in_c = axis_masks((1, 128))
    for tok in range(4):
        at = (batch * 4 + tok) * tiles
        here = iota((256, 1), 0) // 64 == tok
        u = dot(lat, jnp.where(here, wk, 0.0).astype(BF16))
        k = u[:, 0:128] * c + u[:, 128:256] * s
        shift = jnp.where(in_r, float(tok // 2), 0.0) + jnp.where(in_c, float(tok % 2), 0.0)
        keys_ref[at : at + tiles, 0:128] = dead
        keys_ref[at : at + tiles, 128:256] = k.astype(BF16)
        keys_ref[at : at + tiles, 256:384] = (k * (pos + shift)).astype(BF16)
        vals_ref[at : at + tiles, :] = dot(lat, jnp.where(here, wv, 0.0).astype(BF16)).astype(BF16)


def project_queries(lat, fields, tables, wq):
    slots = lat.shape[0]
    tokens = 4 * slots
    taken = (iota((tokens, slots), 0) // 4).astype(F32) == fields[0:1, :].astype(F32)
    chosen = one_hot(taken & (fields[4:5, :].astype(F32) > 0.5))
    which = iota((tokens, 256), 0) % 4 == iota((tokens, 256), 1) // 64
    my_lat = jnp.where(which, dot(chosen, lat), 0.0).astype(BF16)
    my_fields = dot_nt(fields, chosen).astype(BF16)
    s, c, pos = from_fields(my_fields, tables)
    pick = one_hot(iota((FIELDS, META), 0) == 4)
    live = dot_tn(my_fields, pick)
    u = dot(my_lat, wq.astype(BF16))
    q = u[:, 0:128] * c + u[:, 128:256] * s
    in_f, in_r, in_c = axis_masks((tokens, 128))
    tok = iota((tokens, 128), 0) % 4
    pos = pos + jnp.where(in_r & (tok >= 2), 1.0, 0.0) + jnp.where(in_c & (tok % 2 == 1), 1.0, 0.0)
    lane0 = one_hot(iota((tokens, META), 1) == 0)
    scale = 128.0 ** (-0.5) * math.log2(math.e)
    q_ext = jnp.concatenate([lane0, (q * scale).astype(BF16)], axis=1)
    return q, q_ext, pos, live


def finish_attention(q, q_ext, pos, live, top, cot_ref, out_ref, keys_ref, vals_ref, score_ref):
    tokens = q.shape[0]
    keys = keys_ref.shape[0]
    chunk = min(512, keys)
    starts = range(0, keys, chunk)
    top = jnp.max(top, axis=1, keepdims=True)
    sums = jnp.zeros((tokens, chunk), F32)
    mixed = jnp.zeros((tokens, 128), F32)
    for at in starts:
        weights = jnp.exp2(score_ref[:, at : at + chunk] - top)
        score_ref[:, at : at + chunk] = weights
        sums = sums + weights
        mixed = mixed + dot(weights.astype(BF16), vals_ref[at : at + chunk, :])
    inv = 1.0 / jnp.sum(sums, axis=1, keepdims=True)
    mixed = mixed * inv
    out_ref[...] = mixed * live
    cot = cot_ref[...]
    mean = jnp.sum(cot.astype(F32) * mixed, axis=1, keepdims=True)
    back = jnp.zeros((tokens, 256), F32)
    for at in starts:
        dprob = dot_nt(cot, vals_ref[at : at + chunk, :])
        dscore = score_ref[:, at : at + chunk] * (dprob - mean)
        back = back + dot(dscore.astype(BF16), keys_ref[at : at + chunk, 128:384])
    g = pltpu.roll(back[:, 0:128], 64, axis=1)
    gp = pltpu.roll(back[:, 128:256], 64, axis=1)
    terms = q * (pos * g - gp) * (inv * 128.0 ** (-0.5) * live)
    line = jnp.sum(terms, axis=0, keepdims=True)
    other = pltpu.roll(line, 64, axis=1)
    return jnp.where(iota((1, 128), 1) < 64, line - other, other - line)


def greet(axis):
    me_dp, me_seq = lax.axis_index("dp"), lax.axis_index("seq")
    n, me = lax.axis_size(axis), lax.axis_index(axis)
    barrier = pltpu.get_barrier_semaphore()
    for i in sorted(range(1, n), key=lambda i: -min(i, n - i)):
        peer = lax.rem(me + i, n)
        where = (peer, me_seq) if axis == "dp" else (me_dp, peer)
        pl.semaphore_signal(barrier, inc=1, device_id=where, device_id_type=MESH)
    return n - 1


def spread(axis, src_of, dst_ref, send_sem, recv_sem):
    me_dp, me_seq = lax.axis_index("dp"), lax.axis_index("seq")
    n = lax.axis_size(axis)
    me = lax.axis_index(axis)

    def copy(peer, source, target):
        return pltpu.make_async_remote_copy(
            src_ref=source,
            dst_ref=target,
            send_sem=send_sem,
            recv_sem=recv_sem,
            device_id=(peer, me_seq) if axis == "dp" else (me_dp, peer),
            device_id_type=MESH,
        )

    def start():
        for i in range(1, n):
            peer = lax.rem(me + i, n)
            copy(peer, src_of(peer), dst_ref.at[me]).start()

    others = dst_ref.at[pl.ds(0, n - 1)]

    def wait_recv():
        copy(lax.rem(me + 1, n), others, others).wait_recv()

    def wait_send():
        copy(lax.rem(me + 1, n), others, others).wait_send()

    return start, wait_recv, wait_send


def fold_load(embed_ref, qkv_ref, unit, window, columns, sems):
    shard = qkv_ref.shape[0]
    wide = window.shape[1]
    first = (lax.axis_index("seq") * shard) // 128 * 128
    rows = pl.ds(pl.multiple_of(8 * (unit // 3), 8), 8)
    cols = pl.ds(pl.multiple_of(128 * (unit % 3), 128), 128)
    left = pltpu.make_async_copy(embed_ref.at[rows, pl.ds(pl.multiple_of(first, 128), wide)], window, sems.at[0])
    right = pltpu.make_async_copy(qkv_ref.at[:, cols], columns, sems.at[1])
    left.start()
    right.start()
    return left, right


def fold_partial(window, columns):
    shard = columns.shape[0]
    wide = window.shape[1]
    part = window[...].astype(F32)
    if wide != shard:
        odd = lax.axis_index("seq") % 2 == 1
        part = jnp.where(odd, pltpu.roll(part, wide - 64, axis=1), part)
    return dot(part[:, 0:shard].astype(BF16), columns[...])


def turn_weights(source, chans, tap, target):
    part = source[:, tap * chans : (tap + 1) * chans].astype(F32)
    target[0:chans, :] = part.T.astype(BF16)
    rest = target.shape[0] - chans
    if rest:
        target[chans:, :] = jnp.zeros((rest, chans), BF16)


def whole_kernel(
    tiles_hbm,
    dest_hbm,
    meta_hbm,
    space_hbm,
    time_hbm,
    bias_hbm,
    latent_hbm,
    embed_hbm,
    qkv_hbm,
    freq_hbm,
    cot_hbm,
    out_ref,
    grad_ref,
    tiles,
    dest,
    meta,
    space_raw,
    time_raw,
    bias,
    latent,
    freq_in,
    cot,
    window,
    columns,
    load_sem,
    tile_sem,
    fold_sem,
    space,
    time,
    messages,
    arrived,
    blocks,
    fields,
    parts,
    unit_buf,
    unit_all,
    ew,
    keys_ref,
    vals_ref,
    score_ref,
    line,
    mid,
    by_seq,
    by_dp,
    part_send,
    part_recv,
    unit_send,
    unit_recv,
    msg_send,
    msg_recv,
    ring_send,
    ring_recv,
    seq_send,
    seq_recv,
    dp_send,
    dp_recv,
):
    me_dp, me_seq = lax.axis_index("dp"), lax.axis_index("seq")
    n_dp, n_seq = lax.axis_size("dp"), lax.axis_size("seq")
    held, _, height, width, chans = tiles.shape
    per = parts.shape[1]

    count = greet("seq")
    loads = []
    pairs = [(dest_hbm, dest), (meta_hbm, meta), (space_hbm, space_raw), (time_hbm, time_raw), (bias_hbm, bias)]
    pairs += [(latent_hbm, latent), (freq_hbm, freq_in), (cot_hbm, cot)]
    for i, (source, target) in enumerate(pairs):
        loads.append(pltpu.make_async_copy(source, target, load_sem.at[i]))
        loads[-1].start()
    folds = []
    for j in range(per):
        unit = lax.rem(me_dp * per + j, UNITS)
        folds.append(fold_load(embed_hbm, qkv_hbm, unit, window.at[j], columns.at[j], fold_sem.at[j]))
    chunks = []
    for i in range(height // 2):
        rows = pl.ds(2 * i, 2)
        chunks.append(pltpu.make_async_copy(tiles_hbm.at[:, :, rows], tiles.at[:, :, rows], tile_sem.at[i]))
        chunks[-1].start()
    count += greet("dp")

    for load in loads:
        load.wait()
    slot_row, ranked = place_tiles(dest, meta, n_dp)
    picks = packing(slot_row, held * width, width, n_dp)
    deep = space.shape[1] // 3
    for tap in range(9):
        turn_weights(space_raw, chans, tap, space.at[tap % 3, pl.ds(deep * (tap // 3), deep)])
    for tap in (1, 2):
        turn_weights(time_raw, chans, tap, time.at[tap - 1])
    latent_wide = jnp.concatenate([latent[...]] * 16, axis=0)

    start_parts, recv_parts, sent_parts = spread("seq", lambda peer: parts.at[me_seq], parts, part_send, part_recv)
    start_msgs, recv_msgs, sent_msgs = spread("dp", lambda peer: messages.at[peer], arrived, msg_send, msg_recv)
    start_units, recv_units, sent_units = spread("dp", lambda peer: unit_buf, unit_all, unit_send, unit_recv)
    start_seq, recv_seq, sent_seq = spread("seq", lambda peer: line, by_seq, seq_send, seq_recv)
    start_dp, recv_dp, sent_dp = spread("dp", lambda peer: mid, by_dp, dp_send, dp_recv)

    total = None
    for h in range(height // 2):
        if h == 0:
            chunks[0].wait()
        if h + 1 < height // 2:
            chunks[h + 1].wait()
        part = encode_rows(h, tiles, space, time, bias[...], latent_wide)
        total = part if total is None else total + part
    pack_messages(total, picks, ranked, messages)
    pl.semaphore_wait(pltpu.get_barrier_semaphore(), count)
    start_msgs()
    for left, right in folds:
        left.wait()
        right.wait()
    for j in range(per):
        parts[me_seq, j] = fold_partial(window.at[j], columns.at[j])
    start_parts()
    arrived[me_dp] = messages[me_dp]
    recv_msgs()
    unpack_messages(arrived[...], blocks.at[0], fields.at[0])

    far = {1: n_seq // 2, -1: (n_seq - 1) // 2}

    def slot_at(way, distance):
        return 2 * distance - 1 if way == 1 else 2 * distance

    def hop(way, source, distance, links):
        to = lax.rem(me_seq + way * links + n_seq, n_seq)
        slot = slot_at(way, distance)
        copies = []
        for kind, buf in enumerate((blocks, fields)):
            copies.append(
                pltpu.make_async_remote_copy(
                    src_ref=buf.at[source],
                    dst_ref=buf.at[slot],
                    send_sem=ring_send.at[kind, slot],
                    recv_sem=ring_recv.at[kind, slot],
                    device_id=(me_dp, to),
                    device_id_type=MESH,
                )
            )
        return copies

    sends = []

    def send(way, source, distance, links):
        for copy in hop(way, source, distance, links):
            copy.start()
            sends.append(copy)

    def receive(distance):
        for way in (1, -1):
            if distance <= far[way]:
                for copy in hop(way, 0, distance, 1):
                    copy.wait_recv()
                if distance + STRIDE <= far[way]:
                    send(way, slot_at(way, distance), distance + STRIDE, STRIDE)

    for distance in range(1, STRIDE + 1):
        for way in (1, -1):
            if distance <= far[way]:
                send(way, 0, distance, distance)

    recv_parts()
    unit_buf[...] = jnp.sum(parts[...], axis=0)
    unit_all[me_dp] = unit_buf[...]
    start_units()

    group = min(4, n_seq)
    slots = blocks.shape[1]
    tokens = 4 * slots
    last = (n_seq // group - 1) * group
    got = 1
    while slot_at(-1, got) < last or slot_at(1, got) < last:
        receive(got)
        got += 1
    recv_units()
    for unit in range(UNITS):
        ew[8 * (unit // 3) : 8 * (unit // 3) + 8, 128 * (unit % 3) : 128 * (unit % 3) + 128] = unit_all[unit // per, unit % per]

    freq = jnp.concatenate([freq_in[...], freq_in[...]], axis=1)
    tables = rotary_tables(freq)
    wq = token_weights(ew, freq, 0)
    wk = token_weights(ew, freq, 128)
    wv = jnp.concatenate([ew[:, 256:384]] * 4, axis=0)
    q, q_ext, pos, live = project_queries(blocks[0], fields[0, :, 0:slots], tables, wq)
    step = group * tokens
    top = jnp.full((tokens, step), -jnp.inf, F32)
    for batch in range(n_seq // group):
        if batch == n_seq // group - 1:
            while got <= far[1]:
                receive(got)
                got += 1
        part = pl.ds(batch * group, group)
        project_keys(batch, blocks.at[part], fields.at[part], tables, wk, wv, keys_ref, vals_ref)
        scores = dot_nt(q_ext, keys_ref[batch * step : (batch + 1) * step, 0:256])
        score_ref[:, batch * step : (batch + 1) * step] = scores
        top = jnp.maximum(top, scores)
    line[...] = finish_attention(q, q_ext, pos, live, top, cot, out_ref, keys_ref, vals_ref, score_ref)

    start_seq()
    by_seq[me_seq] = line[...]
    recv_seq()
    mid[...] = jnp.sum(by_seq[...], axis=0)
    start_dp()
    by_dp[me_dp] = mid[...]
    for copy in sends:
        copy.wait_send()
    sent_msgs()
    sent_parts()
    sent_units()
    sent_seq()
    recv_dp()
    grad_ref[...] = jnp.sum(by_dp[...], axis=0)[:, 0 : grad_ref.shape[1]]
    sent_dp()


def per_device(
    tiles,
    tile_dest,
    tile_meta,
    space_weight,
    time_weight,
    conv_bias,
    latent_weight,
    embed_weight,
    qkv_weight,
    rope_freq,
    cotangent,
):
    n_dp, n_seq = lax.axis_size("dp"), lax.axis_size("seq")
    chans = tiles.shape[-1]
    slots = 2 * n_dp
    tokens = 4 * slots
    keys = tokens * n_seq
    per = -(-UNITS // n_dp)
    shard = qkv_weight.shape[0]
    pairs = rope_freq.shape[0]
    operands = (
        tiles,
        tile_dest[None, :],
        tile_meta.T,
        space_weight.T,
        time_weight.T,
        conv_bias[None, :],
        latent_weight.T,
        embed_weight,
        qkv_weight,
        rope_freq[None, :],
        cotangent,
    )
    dma = pltpu.SemaphoreType.DMA
    buf = pltpu.VMEM
    local = [operands[i] for i in (0, 1, 2, 3, 4, 5, 6, 9, 10)]
    scratch = [buf(a.shape, a.dtype) for a in local]
    scratch += [
        buf((per, 8, -(-shard // 128) * 128), BF16),
        buf((per, shard, 128), BF16),
        dma((8,)),
        dma((tiles.shape[2] // 2,)),
        dma((per, 2)),
        buf((3, 3 * 256, chans), BF16),
        buf((2, chans, chans), BF16),
        buf((n_dp, 8, 128), BF16),
        buf((n_dp, 8, 128), BF16),
        buf((n_seq, slots, 256), BF16),
        buf((n_seq, FIELDS, META), BF16),
        buf((n_seq, per, 8, 128), F32),
        buf((per, 8, 128), F32),
        buf((n_dp, per, 8, 128), F32),
        buf((64, 384), F32),
        buf((keys, 384), BF16),
        buf((keys, 128), BF16),
        buf((tokens, keys), F32),
        buf((1, 128), F32),
        buf((1, 128), F32),
        buf((n_seq, 1, 128), F32),
        buf((n_dp, 1, 128), F32),
        dma(()),
        dma(()),
        dma(()),
        dma(()),
        dma(()),
        dma(()),
        dma((2, n_seq)),
        dma((2, n_seq)),
        dma(()),
        dma(()),
        dma(()),
        dma(()),
    ]
    vmem = pl.BlockSpec(memory_space=pltpu.VMEM)
    attended, grad = pl.pallas_call(
        whole_kernel,
        out_shape=(
            jax.ShapeDtypeStruct((tokens, 128), F32),
            jax.ShapeDtypeStruct((1, pairs), F32),
        ),
        in_specs=[pl.BlockSpec(memory_space=pltpu.HBM)] * len(operands),
        out_specs=(vmem, vmem),
        scratch_shapes=scratch,
        compiler_params=pltpu.CompilerParams(
            vmem_limit_bytes=24 << 20, collective_id=0, has_side_effects=True
        ),
    )(*[pltpu.with_memory_space_constraint(a, pltpu.HBM) for a in operands])
    return attended.astype(BF16), grad[0]


def solution(mesh):
    both = ("dp", "seq")
    specs = (
        P(both, None, None, None, None),
        P(both),
        P(both, None),
        P(),
        P(),
        P(),
        P(),
        P(),
        P("seq", None),
        P(),
        P(both, None),
    )
    return jax.shard_map(
        per_device,
        mesh=mesh,
        in_specs=specs,
        out_specs=(P(both, None), P()),
        check_vma=False,
    )
```

```python
import math

import jax
import jax.numpy as jnp
from jax import lax
from jax.experimental import pallas as pl
from jax.experimental.pallas import tpu as pltpu
from jax.sharding import PartitionSpec as P

F32 = jnp.float32
BF16 = jnp.bfloat16
MESH = pl.DeviceIdType.MESH
META = 128
BIG = 1e30
UNITS = 24
FIELDS = 8
STRIDE = 2


def iota(shape, dim):
    return lax.broadcasted_iota(jnp.int32, shape, dim)


def dot(a, b):
    return jnp.dot(a, b, preferred_element_type=F32)


def dot_nt(a, b):
    return lax.dot_general(a, b, (((1,), (1,)), ((), ())), preferred_element_type=F32)


def dot_tn(a, b):
    return lax.dot_general(a, b, (((0,), (0,)), ((), ())), preferred_element_type=F32)


def one_hot(cond):
    return jnp.where(cond, 1.0, 0.0).astype(BF16)


def place_tiles(dest_ref, meta_ref, owners):
    held = dest_ref.shape[1]
    square = (held, held)
    row = jnp.broadcast_to(dest_ref[...].astype(F32), square)
    first, second = iota(square, 0), iota(square, 1)
    col = jnp.sum(jnp.where(first == second, row, 0.0), axis=1, keepdims=True)
    same = jnp.where(col == row, 1.0, 0.0)
    rank_row = jnp.sum(jnp.where(first < second, same, 0.0), axis=0, keepdims=True)
    rank_col = jnp.sum(jnp.where(second < first, same, 0.0), axis=1, keepdims=True)
    slot_row = 2.0 * row[0:1, :] + rank_row
    shape = (8, held)
    fields = jnp.concatenate([meta_ref[...].astype(F32), jnp.ones((4, held), F32)], axis=0)
    fields = jnp.where(iota(shape, 0) < 5, fields, 0.0).astype(BF16)
    pick = one_hot(iota((8, META), 0) == iota((8, META), 1) % 8)
    lanes = dot_tn(fields, pick)
    ranked = jnp.where((iota((held, META), 1) // 8).astype(F32) == rank_col, lanes, 0.0).astype(BF16)
    return slot_row, ranked


def encode_rows(h, tiles_ref, space_ref, time_ref, bias, latent):
    held, frames, height, width, chans = tiles_ref.shape
    rows = held * width
    lat_wide = latent.shape[0]
    deep = space_ref.shape[1] // 3
    pad = jnp.zeros((held * frames * width, deep - chans), BF16)
    taps = []
    for src in range(2 * h, min(2 * h + 3, height)):
        taps += [tiles_ref[:, :, src].reshape(held * frames * width, chans), pad]
    x = jnp.concatenate(taps, axis=1)
    shifted = [dot(x, space_ref[col_off, 0 : x.shape[1], :]) for col_off in range(3)]
    y0, y1, y2 = [y.reshape(held * frames, width, chans) for y in shifted]
    y1 = pltpu.roll(y1, width - 1, axis=1)
    edge = iota((1, width, chans), 1) < width - 2
    y2 = jnp.where(edge, pltpu.roll(y2, width - 2, axis=1), 0.0)
    spatial = (y0 + y1 + y2).reshape(held, frames, width, chans)
    first = spatial[:, 0].reshape(rows, chans).astype(BF16)
    second = spatial[:, 1].reshape(rows, chans).astype(BF16)
    summed = dot(first, time_ref[0]) + dot(second, time_ref[1]) + bias
    feats = (summed / (1.0 + jnp.exp(-summed))).astype(BF16)
    lane = iota((rows, lat_wide), 1)
    lane_h = 2 * (lane // 128) + (lane // 32) % 2
    lane_w = 2 * ((lane // 64) % 2) + (lane // 16) % 2
    keep = (lane_h == h) & (2 * lane_w == iota((rows, lat_wide), 0) % width)
    return jnp.where(keep, dot_nt(feats, latent), 0.0)


def packing(slot_row, rows, width, owners):
    held = slot_row.shape[1]
    shape = (8 * owners, held)
    sub = iota(shape, 0) % 8
    mine = (2 * (iota(shape, 0) // 8) + sub // 2).astype(F32) == slot_row
    hit = one_hot(mine & (sub < 4))
    wide = dot(hit, one_hot(iota((held, rows), 0) == iota((held, rows), 1) // width))
    even = iota((8 * owners, rows), 0) % 2 == 0
    owner = jnp.floor(slot_row * 0.5)
    named = one_hot(((iota(shape, 0) // 8).astype(F32) == owner) & (sub == 4))
    return jnp.where(even, wide, 0.0).astype(BF16), jnp.where(even, 0.0, wide).astype(BF16), named


def pack_messages(latents, picks, ranked, out_ref):
    owners = out_ref.shape[0]
    latents = latents.astype(BF16)
    packed = dot(picks[0], latents[:, 0:128]) + dot(picks[1], latents[:, 128:256]) + dot(picks[2], ranked)
    out_ref[...] = packed.astype(BF16).reshape(owners, 8, 128)


def unpack_messages(arrived, block_ref, field_ref):
    loaders = arrived.shape[0]
    slots = 2 * loaders
    flat = arrived.reshape(8 * loaders, 128)
    shape = (slots, 8 * loaders)
    base = 8 * (iota(shape, 0) // 2) + 2 * (iota(shape, 0) % 2)
    block_ref[:, 0:128] = dot(one_hot(iota(shape, 1) == base), flat).astype(BF16)
    block_ref[:, 128:256] = dot(one_hot(iota(shape, 1) == base + 1), flat).astype(BF16)
    both = dot(one_hot(iota(shape, 1) == 8 * (iota(shape, 0) // 2) + 4), flat)
    odd = iota((slots, META), 0) % 2 == 1
    fields = jnp.where(odd, pltpu.roll(both, META - 8, axis=1), both)
    pick = one_hot(iota((8, META), 0) == iota((8, META), 1))
    turned = dot_nt(pick, fields.astype(BF16))
    wide = jnp.concatenate([turned, jnp.zeros((8, META - slots), F32)], axis=1)
    field_ref[...] = wide.astype(BF16)


def sincos(angle):
    turns = jnp.floor(angle * (0.5 / math.pi) + 0.5)
    r = angle - turns * 6.28125
    r = r - turns * (2.0 * math.pi - 6.28125)
    z = r * r
    s = jnp.full_like(z, -1.0 / math.factorial(15))
    for n in (13, 11, 9, 7, 5, 3, 1):
        s = s * z + (1.0 if n % 4 == 1 else -1.0) / math.factorial(n)
    c = jnp.full_like(z, 1.0 / math.factorial(16))
    for n in (14, 12, 10, 8, 6, 4, 2, 0):
        c = c * z + (1.0 if n % 4 == 0 else -1.0) / math.factorial(n)
    return s * r, c


def axis_masks(shape):
    pair = iota(shape, 1) % 64
    return pair < 22, (pair >= 22) & (pair < 43), pair >= 43


def swap_halves(u):
    lane = iota(u.shape, 1)
    turned = pltpu.roll(u, 64, axis=1)
    return jnp.where(lane < 64, -turned, turned)


def rotary_tables(freq):
    shape = (FIELDS, META)
    sub = iota(shape, 0)
    in_f, in_r, in_c = axis_masks(shape)
    step = jnp.where((sub == 1) & in_f, 1.0, 0.0)
    step = jnp.where(((sub == 2) & in_r) | ((sub == 3) & in_c), 2.0, step)
    rest = jnp.broadcast_to(freq, shape)
    tables = []
    for _ in range(3):
        part = rest.astype(BF16).astype(F32)
        rest = rest - part
        tables.append((step * part).astype(BF16))
    return jnp.concatenate(tables + [step.astype(BF16)], axis=1)


def token_weights(ew_ref, freq, first):
    base = ew_ref[:, first : first + 128]
    shape = (8, 128)
    in_f, in_r, in_c = axis_masks(shape)
    blocks = []
    for tok in range(4):
        offset = jnp.where(in_r, float(tok // 2), 0.0) + jnp.where(in_c, float(tok % 2), 0.0)
        s, c = sincos(jnp.broadcast_to(freq, shape) * offset)
        turned = base * c[0:1, :] + swap_halves(base) * s[0:1, :]
        blocks.append(jnp.concatenate([turned, swap_halves(turned)], axis=1))
    return jnp.concatenate(blocks, axis=0)


def from_fields(fields, tables):
    wide = dot_tn(fields, tables)
    angle = wide[:, 0:128] + wide[:, 128:256] + wide[:, 256:384]
    s, c = sincos(angle)
    return s, c, wide[:, 384:512]


def project_keys(batch, block_ref, field_ref, tables, wk, wv, keys_ref, vals_ref):
    blocks, slots, _ = block_ref.shape
    tiles = blocks * slots
    wide = [dot_tn(field_ref[i, :, 0:slots], tables) for i in range(blocks)]
    wide = jnp.concatenate(wide, axis=0)
    s, c = sincos(wide[:, 0:128] + wide[:, 128:256] + wide[:, 256:384])
    pos = wide[:, 384:512]
    pick = one_hot((iota((FIELDS, META), 0) == 4) & (iota((FIELDS, META), 1) == 0))
    live = jnp.concatenate([dot_tn(field_ref[i, :, 0:slots], pick) for i in range(blocks)], axis=0)
    dead = jnp.where(iota((tiles, META), 1) == 0, (live - 1.0) * BIG, 0.0).astype(BF16)
    lat = block_ref[...].reshape(tiles, 256)
    in_f, in_r, in_c = axis_masks((1, 128))
    for tok in range(4):
        at = (batch * 4 + tok) * tiles
        here = iota((256, 1), 0) // 64 == tok
        u = dot(lat, jnp.where(here, wk, 0.0).astype(BF16))
        k = u[:, 0:128] * c + u[:, 128:256] * s
        shift = jnp.where(in_r, float(tok // 2), 0.0) + jnp.where(in_c, float(tok % 2), 0.0)
        keys_ref[at : at + tiles, 0:128] = dead
        keys_ref[at : at + tiles, 128:256] = k.astype(BF16)
        keys_ref[at : at + tiles, 256:384] = (k * (pos + shift)).astype(BF16)
        vals_ref[at : at + tiles, :] = dot(lat, jnp.where(here, wv, 0.0).astype(BF16)).astype(BF16)


def project_queries(lat, fields, tables, wq):
    slots = lat.shape[0]
    tokens = 4 * slots
    taken = (iota((tokens, slots), 0) // 4).astype(F32) == fields[0:1, :].astype(F32)
    chosen = one_hot(taken & (fields[4:5, :].astype(F32) > 0.5))
    which = iota((tokens, 256), 0) % 4 == iota((tokens, 256), 1) // 64
    my_lat = jnp.where(which, dot(chosen, lat), 0.0).astype(BF16)
    my_fields = dot_nt(fields, chosen).astype(BF16)
    s, c, pos = from_fields(my_fields, tables)
    pick = one_hot(iota((FIELDS, META), 0) == 4)
    live = dot_tn(my_fields, pick)
    u = dot(my_lat, wq.astype(BF16))
    q = u[:, 0:128] * c + u[:, 128:256] * s
    in_f, in_r, in_c = axis_masks((tokens, 128))
    tok = iota((tokens, 128), 0) % 4
    pos = pos + jnp.where(in_r & (tok >= 2), 1.0, 0.0) + jnp.where(in_c & (tok % 2 == 1), 1.0, 0.0)
    lane0 = one_hot(iota((tokens, META), 1) == 0)
    scale = 128.0 ** (-0.5) * math.log2(math.e)
    q_ext = jnp.concatenate([lane0, (q * scale).astype(BF16)], axis=1)
    return q, q_ext, pos, live


def finish_attention(q, q_ext, pos, live, top, cot_ref, out_ref, keys_ref, vals_ref, score_ref):
    tokens = q.shape[0]
    keys = keys_ref.shape[0]
    chunk = min(512, keys)
    starts = range(0, keys, chunk)
    top = jnp.max(top, axis=1, keepdims=True)
    sums = jnp.zeros((tokens, chunk), F32)
    mixed = jnp.zeros((tokens, 128), F32)
    for at in starts:
        weights = jnp.exp2(score_ref[:, at : at + chunk] - top)
        score_ref[:, at : at + chunk] = weights
        sums = sums + weights
        mixed = mixed + dot(weights.astype(BF16), vals_ref[at : at + chunk, :])
    inv = 1.0 / jnp.sum(sums, axis=1, keepdims=True)
    mixed = mixed * inv
    out_ref[...] = mixed * live
    cot = cot_ref[...]
    mean = jnp.sum(cot.astype(F32) * mixed, axis=1, keepdims=True)
    back = jnp.zeros((tokens, 256), F32)
    for at in starts:
        dprob = dot_nt(cot, vals_ref[at : at + chunk, :])
        dscore = score_ref[:, at : at + chunk] * (dprob - mean)
        back = back + dot(dscore.astype(BF16), keys_ref[at : at + chunk, 128:384])
    g = pltpu.roll(back[:, 0:128], 64, axis=1)
    gp = pltpu.roll(back[:, 128:256], 64, axis=1)
    terms = q * (pos * g - gp) * (inv * 128.0 ** (-0.5) * live)
    line = jnp.sum(terms, axis=0, keepdims=True)
    other = pltpu.roll(line, 64, axis=1)
    return jnp.where(iota((1, 128), 1) < 64, line - other, other - line)


def greet(axis):
    me_dp, me_seq = lax.axis_index("dp"), lax.axis_index("seq")
    n, me = lax.axis_size(axis), lax.axis_index(axis)
    barrier = pltpu.get_barrier_semaphore()
    for i in sorted(range(1, n), key=lambda i: -min(i, n - i)):
        peer = lax.rem(me + i, n)
        where = (peer, me_seq) if axis == "dp" else (me_dp, peer)
        pl.semaphore_signal(barrier, inc=1, device_id=where, device_id_type=MESH)
    return n - 1


def spread(axis, src_of, dst_ref, send_sem, recv_sem):
    me_dp, me_seq = lax.axis_index("dp"), lax.axis_index("seq")
    n = lax.axis_size(axis)
    me = lax.axis_index(axis)

    def copy(peer, source, target):
        return pltpu.make_async_remote_copy(
            src_ref=source,
            dst_ref=target,
            send_sem=send_sem,
            recv_sem=recv_sem,
            device_id=(peer, me_seq) if axis == "dp" else (me_dp, peer),
            device_id_type=MESH,
        )

    def start():
        for i in range(1, n):
            peer = lax.rem(me + i, n)
            copy(peer, src_of(peer), dst_ref.at[me]).start()

    others = dst_ref.at[pl.ds(0, n - 1)]

    def wait_recv():
        copy(lax.rem(me + 1, n), others, others).wait_recv()

    def wait_send():
        copy(lax.rem(me + 1, n), others, others).wait_send()

    return start, wait_recv, wait_send


def fold_load(embed_ref, qkv_ref, unit, window, columns, sems):
    shard = qkv_ref.shape[0]
    wide = window.shape[1]
    first = (lax.axis_index("seq") * shard) // 128 * 128
    rows = pl.ds(pl.multiple_of(8 * (unit // 3), 8), 8)
    cols = pl.ds(pl.multiple_of(128 * (unit % 3), 128), 128)
    left = pltpu.make_async_copy(embed_ref.at[rows, pl.ds(pl.multiple_of(first, 128), wide)], window, sems.at[0])
    right = pltpu.make_async_copy(qkv_ref.at[:, cols], columns, sems.at[1])
    left.start()
    right.start()
    return left, right


def fold_partial(window, columns):
    shard = columns.shape[0]
    wide = window.shape[1]
    part = window[...].astype(F32)
    if wide != shard:
        odd = lax.axis_index("seq") % 2 == 1
        part = jnp.where(odd, pltpu.roll(part, wide - 64, axis=1), part)
    return dot(part[:, 0:shard].astype(BF16), columns[...])


def turn_weights(source, chans, tap, target):
    part = source[:, tap * chans : (tap + 1) * chans].astype(F32)
    target[0:chans, :] = part.T.astype(BF16)
    rest = target.shape[0] - chans
    if rest:
        target[chans:, :] = jnp.zeros((rest, chans), BF16)


def whole_kernel(
    tiles_hbm,
    dest_hbm,
    meta_hbm,
    space_hbm,
    time_hbm,
    bias_hbm,
    latent_hbm,
    embed_hbm,
    qkv_hbm,
    freq_hbm,
    cot_hbm,
    out_ref,
    grad_ref,
    tiles,
    dest,
    meta,
    space_raw,
    time_raw,
    bias,
    latent,
    freq_in,
    cot,
    window,
    columns,
    load_sem,
    tile_sem,
    fold_sem,
    space,
    time,
    messages,
    arrived,
    blocks,
    fields,
    parts,
    unit_buf,
    unit_all,
    ew,
    keys_ref,
    vals_ref,
    score_ref,
    line,
    mid,
    by_seq,
    by_dp,
    part_send,
    part_recv,
    unit_send,
    unit_recv,
    msg_send,
    msg_recv,
    ring_send,
    ring_recv,
    seq_send,
    seq_recv,
    dp_send,
    dp_recv,
):
    me_dp, me_seq = lax.axis_index("dp"), lax.axis_index("seq")
    n_dp, n_seq = lax.axis_size("dp"), lax.axis_size("seq")
    held, _, height, width, chans = tiles.shape
    per = parts.shape[1]

    count = greet("seq")
    loads = []
    pairs = [(dest_hbm, dest), (meta_hbm, meta), (space_hbm, space_raw), (time_hbm, time_raw), (bias_hbm, bias)]
    pairs += [(latent_hbm, latent), (freq_hbm, freq_in), (cot_hbm, cot)]
    for i, (source, target) in enumerate(pairs):
        loads.append(pltpu.make_async_copy(source, target, load_sem.at[i]))
        loads[-1].start()
    folds = []
    for j in range(per):
        unit = lax.rem(me_dp * per + j, UNITS)
        folds.append(fold_load(embed_hbm, qkv_hbm, unit, window.at[j], columns.at[j], fold_sem.at[j]))
    chunks = []
    for i in range(height // 2):
        rows = pl.ds(2 * i, 2)
        chunks.append(pltpu.make_async_copy(tiles_hbm.at[:, :, rows], tiles.at[:, :, rows], tile_sem.at[i]))
        chunks[-1].start()
    count += greet("dp")

    for load in loads[0:2]:
        load.wait()
    slot_row, ranked = place_tiles(dest, meta, n_dp)
    picks = packing(slot_row, held * width, width, n_dp)
    for load in loads[2:]:
        load.wait()
    deep = space.shape[1] // 3
    for tap in range(9):
        turn_weights(space_raw, chans, tap, space.at[tap % 3, pl.ds(deep * (tap // 3), deep)])
    for tap in (1, 2):
        turn_weights(time_raw, chans, tap, time.at[tap - 1])
    latent_wide = jnp.concatenate([latent[...]] * 16, axis=0)

    start_parts, recv_parts, sent_parts = spread("seq", lambda peer: parts.at[me_seq], parts, part_send, part_recv)
    start_msgs, recv_msgs, sent_msgs = spread("dp", lambda peer: messages.at[peer], arrived, msg_send, msg_recv)
    start_units, recv_units, sent_units = spread("dp", lambda peer: unit_buf, unit_all, unit_send, unit_recv)
    start_seq, recv_seq, sent_seq = spread("seq", lambda peer: line, by_seq, seq_send, seq_recv)
    start_dp, recv_dp, sent_dp = spread("dp", lambda peer: mid, by_dp, dp_send, dp_recv)

    total = None
    for h in range(height // 2):
        if h == 0:
            chunks[0].wait()
        if h + 1 < height // 2:
            chunks[h + 1].wait()
        part = encode_rows(h, tiles, space, time, bias[...], latent_wide)
        total = part if total is None else total + part
    pack_messages(total, picks, ranked, messages)
    pl.semaphore_wait(pltpu.get_barrier_semaphore(), count)
    start_msgs()
    for left, right in folds:
        left.wait()
        right.wait()
    for j in range(per):
        parts[me_seq, j] = fold_partial(window.at[j], columns.at[j])
    start_parts()
    arrived[me_dp] = messages[me_dp]
    recv_msgs()
    unpack_messages(arrived[...], blocks.at[0], fields.at[0])

    far = {1: n_seq // 2, -1: (n_seq - 1) // 2}

    def slot_at(way, distance):
        return 2 * distance - 1 if way == 1 else 2 * distance

    def hop(way, source, distance, links):
        to = lax.rem(me_seq + way * links + n_seq, n_seq)
        slot = slot_at(way, distance)
        copies = []
        for kind, buf in enumerate((blocks, fields)):
            copies.append(
                pltpu.make_async_remote_copy(
                    src_ref=buf.at[source],
                    dst_ref=buf.at[slot],
                    send_sem=ring_send.at[kind, slot],
                    recv_sem=ring_recv.at[kind, slot],
                    device_id=(me_dp, to),
                    device_id_type=MESH,
                )
            )
        return copies

    sends = []

    def send(way, source, distance, links):
        for copy in hop(way, source, distance, links):
            copy.start()
            sends.append(copy)

    def receive(distance):
        for way in (1, -1):
            if distance <= far[way]:
                for copy in hop(way, 0, distance, 1):
                    copy.wait_recv()
                if distance + STRIDE <= far[way]:
                    send(way, slot_at(way, distance), distance + STRIDE, STRIDE)

    for distance in range(1, STRIDE + 1):
        for way in (1, -1):
            if distance <= far[way]:
                send(way, 0, distance, distance)

    recv_parts()
    unit_buf[...] = jnp.sum(parts[...], axis=0)
    unit_all[me_dp] = unit_buf[...]
    start_units()

    group = min(4, n_seq)
    slots = blocks.shape[1]
    tokens = 4 * slots
    last = (n_seq // group - 1) * group
    got = 1
    while slot_at(-1, got) < last or slot_at(1, got) < last:
        receive(got)
        got += 1
    recv_units()
    for unit in range(UNITS):
        ew[8 * (unit // 3) : 8 * (unit // 3) + 8, 128 * (unit % 3) : 128 * (unit % 3) + 128] = unit_all[unit // per, unit % per]

    freq = jnp.concatenate([freq_in[...], freq_in[...]], axis=1)
    tables = rotary_tables(freq)
    wq = token_weights(ew, freq, 0)
    wk = token_weights(ew, freq, 128)
    wv = jnp.concatenate([ew[:, 256:384]] * 4, axis=0)
    q, q_ext, pos, live = project_queries(blocks[0], fields[0, :, 0:slots], tables, wq)
    step = group * tokens
    top = jnp.full((tokens, step), -jnp.inf, F32)
    for batch in range(n_seq // group):
        if batch == n_seq // group - 1:
            while got <= far[1]:
                receive(got)
                got += 1
        part = pl.ds(batch * group, group)
        project_keys(batch, blocks.at[part], fields.at[part], tables, wk, wv, keys_ref, vals_ref)
        scores = dot_nt(q_ext, keys_ref[batch * step : (batch + 1) * step, 0:256])
        score_ref[:, batch * step : (batch + 1) * step] = scores
        top = jnp.maximum(top, scores)
    line[...] = finish_attention(q, q_ext, pos, live, top, cot, out_ref, keys_ref, vals_ref, score_ref)

    start_seq()
    by_seq[me_seq] = line[...]
    recv_seq()
    mid[...] = jnp.sum(by_seq[...], axis=0)
    start_dp()
    by_dp[me_dp] = mid[...]
    for copy in sends:
        copy.wait_send()
    sent_msgs()
    sent_parts()
    sent_units()
    sent_seq()
    recv_dp()
    grad_ref[...] = jnp.sum(by_dp[...], axis=0)[:, 0 : grad_ref.shape[1]]
    sent_dp()


def per_device(
    tiles,
    tile_dest,
    tile_meta,
    space_weight,
    time_weight,
    conv_bias,
    latent_weight,
    embed_weight,
    qkv_weight,
    rope_freq,
    cotangent,
):
    n_dp, n_seq = lax.axis_size("dp"), lax.axis_size("seq")
    chans = tiles.shape[-1]
    slots = 2 * n_dp
    tokens = 4 * slots
    keys = tokens * n_seq
    per = -(-UNITS // n_dp)
    shard = qkv_weight.shape[0]
    pairs = rope_freq.shape[0]
    operands = (
        tiles,
        tile_dest[None, :],
        tile_meta.T,
        space_weight.T,
        time_weight.T,
        conv_bias[None, :],
        latent_weight.T,
        embed_weight,
        qkv_weight,
        rope_freq[None, :],
        cotangent,
    )
    dma = pltpu.SemaphoreType.DMA
    buf = pltpu.VMEM
    local = [operands[i] for i in (0, 1, 2, 3, 4, 5, 6, 9, 10)]
    scratch = [buf(a.shape, a.dtype) for a in local]
    scratch += [
        buf((per, 8, -(-shard // 128) * 128), BF16),
        buf((per, shard, 128), BF16),
        dma((8,)),
        dma((tiles.shape[2] // 2,)),
        dma((per, 2)),
        buf((3, 3 * 256, chans), BF16),
        buf((2, chans, chans), BF16),
        buf((n_dp, 8, 128), BF16),
        buf((n_dp, 8, 128), BF16),
        buf((n_seq, slots, 256), BF16),
        buf((n_seq, FIELDS, META), BF16),
        buf((n_seq, per, 8, 128), F32),
        buf((per, 8, 128), F32),
        buf((n_dp, per, 8, 128), F32),
        buf((64, 384), F32),
        buf((keys, 384), BF16),
        buf((keys, 128), BF16),
        buf((tokens, keys), F32),
        buf((1, 128), F32),
        buf((1, 128), F32),
        buf((n_seq, 1, 128), F32),
        buf((n_dp, 1, 128), F32),
        dma(()),
        dma(()),
        dma(()),
        dma(()),
        dma(()),
        dma(()),
        dma((2, n_seq)),
        dma((2, n_seq)),
        dma(()),
        dma(()),
        dma(()),
        dma(()),
    ]
    vmem = pl.BlockSpec(memory_space=pltpu.VMEM)
    attended, grad = pl.pallas_call(
        whole_kernel,
        out_shape=(
            jax.ShapeDtypeStruct((tokens, 128), F32),
            jax.ShapeDtypeStruct((1, pairs), F32),
        ),
        in_specs=[pl.BlockSpec(memory_space=pltpu.HBM)] * len(operands),
        out_specs=(vmem, vmem),
        scratch_shapes=scratch,
        compiler_params=pltpu.CompilerParams(
            vmem_limit_bytes=24 << 20, collective_id=0, has_side_effects=True
        ),
    )(*[pltpu.with_memory_space_constraint(a, pltpu.HBM) for a in operands])
    return attended.astype(BF16), grad[0]


def solution(mesh):
    both = ("dp", "seq")
    specs = (
        P(both, None, None, None, None),
        P(both),
        P(both, None),
        P(),
        P(),
        P(),
        P(),
        P(),
        P("seq", None),
        P(),
        P(both, None),
    )
    return jax.shard_map(
        per_device,
        mesh=mesh,
        in_specs=specs,
        out_specs=(P(both, None), P()),
        check_vma=False,
    )
```
